32 devices in a mesh: dp: 4 (over z), expert: 8 (over y, x, core).
Axes of the slice: x: 2, y: 2, z: 4, core: 2. Of those that a mesh axis runs over, the one named last changes fastest.
Arguments:
- tokens: bfloat16 [2048, 4096], P(('dp', 'expert')), may hold values from -6 to 6
- queries: bfloat16 [2048, 4096], P(('dp', 'expert')), may hold values from -64 to 64
- keys_values: bfloat16 [2048, 2048], P(('dp', 'expert')), may hold values from -4 to 4
- scan_input: bfloat16 [2048, 4096], P(('dp', 'expert')), may hold values from -6 to 6
- state_maps: float32 [2048, 32], P(('dp', 'expert')), may hold values from -1.5 to 1.5
- step_size: float32 [2048, 64], P(('dp', 'expert')), may hold values from 0.05 to 0.5
- step_decay: float32 [2048, 64], P(('dp', 'expert')), may hold values from -1.2 to 0
- block_pool: bfloat16 [256, 16, 2048], P(('dp', 'expert')), may hold values from -5 to 5
- state_pool: float32 [64, 65536], P(('dp', 'expert')), may hold values from -5 to 5
- block_holder: int32 [32, 16], P(('dp', 'expert')), may hold values from 0 to 3, as said below
- block_index: int32 [32, 16], P(('dp', 'expert')), may hold values from 0 to 7
- cached_blocks: int32 [32], P(('dp', 'expert')), may hold values from 1 to 16, as said below
- state_holder: int32 [32], P(('dp', 'expert')), may hold values from 0 to 3
- state_index: int32 [32], P(('dp', 'expert')), may hold values from 0 to 1
- norm_gain: float32 [4096], replicated, may hold values from 0.1 to 1.9
- router_weight: bfloat16 [4096, 8], replicated, may hold values from -0.09375 to 0.09375
- expert_ids: int32 [2048, 2], P(('dp', 'expert')), may hold values from 0 to 7, all different within a row; in each aligned block of 64 rows (0 to 63, 64 to 127, ...) at most 16 rows name the same one
- up_weight: bfloat16 [8, 4096, 7168], P('expert', None, 'dp'), may hold values from -0.09375 to 0.09375
- down_weight: bfloat16 [8, 7168, 4096], P('expert', 'dp'), may hold values from -0.0625 to 0.0625
Outputs:
- layer_out: bfloat16 [2048, 4096], P(('dp', 'expert'))
- final_state: float32 [32, 65536], P(('dp', 'expert'))
The draws below stay inside these ranges and needn't reach their ends.
Inputs may be any that keep to these rules, and one draw needn't show every extreme that they name: `block_holder`: each row names every holder exactly 4 times over its 16 entries, so at most 4 of a request's cached blocks sit on one holder. `cached_blocks`: some request caches 16 blocks. `expert_ids`: the two experts of a token differ, and each expert is named by exactly 16 rows of one device.
All inputs are finite; a program needn't handle non-finite values.
Results may differ from the reference program's by a relative error of at most 0.0095.
Values may be sent and summed in bfloat16 or wider, within the bound.
No kernel may reach another device: no remote copies, remote signals or barrier semaphores. Data moves between devices by JAX's collectives and lax.ppermute only.
A program may use at most 128 MiB of HBM per device.

```python
import math
import jax
import jax.numpy as jnp
import numpy as np
from jax import lax

D = 4096
HEADS = 32
KV_HEADS = 8
HEAD = 128
SSM_HEADS = 64
SSM_DIM = 64
NSTATE = 16
FF = 7168
BLOCK = 16
MAXB = 16
POOL = 8
SPOOL = 2
SHARD_FRESH_ITEMS = 64
EXPERTS = 8
FF_DEV = 1792
CAP = 16
SLOT = 4
REQS = 32
FRESH_ITEMS_ALL = 2048
N_DP = 4
N_EXPERT = 8
DEVICES = 32


def draw_block_holder(key, part):
    key = jax.random.fold_in(key, 101)
    scores = jax.random.randint(key, (REQS, MAXB), 0, 1 << 20) * MAXB + jnp.arange(MAXB, dtype=jnp.int32)[None, :]
    order = jnp.argsort(scores, axis=1)
    base = jnp.arange(MAXB, dtype=jnp.int32) // SLOT
    return base[order].astype(jnp.int32)


def draw_cached_blocks(key, part):
    first, second = jax.random.split(jax.random.fold_in(key, 202))
    counts = jax.random.randint(first, (REQS,), 1, MAXB + 1)
    picked = jax.random.randint(second, (), 0, REQS)
    return jnp.where(jnp.arange(REQS) == picked, MAXB, counts).astype(jnp.int32)


def attention_inputs(key):
    key = jax.random.fold_in(key, 303)
    lookup_string = jax.random.split(key, 2)
    queries = jnp.clip(jax.random.normal(lookup_string[0], (FRESH_ITEMS_ALL, HEADS * HEAD), jnp.float32), -4.0, 4.0)
    pairs = jnp.clip(jax.random.normal(lookup_string[1], (FRESH_ITEMS_ALL, 2 * KV_HEADS * HEAD), jnp.float32), -4.0, 4.0)
    return (queries, pairs)


def draw_queries(key, part):
    return attention_inputs(key)[0].astype(jnp.bfloat16)


def draw_keys_values(key, part):
    return attention_inputs(key)[1].astype(jnp.bfloat16)


def draw_step_decay(key, part):
    key = jax.random.fold_in(key, 404)
    lookup_string = jax.random.split(key, 5)
    query_group = jnp.arange(FRESH_ITEMS_ALL) // SHARD_FRESH_ITEMS
    lowest, highest = (0.003, 0.12)
    forgetting_speeds = jnp.exp(jax.random.uniform(lookup_string[0], (REQS, SSM_HEADS), jnp.float32, math.log(lowest), math.log(highest)))
    multiplier_value = jnp.exp(jax.random.uniform(lookup_string[1], (REQS,), jnp.float32, math.log(0.5), math.log(2.0)))
    approximate_guess = jnp.exp(jax.random.uniform(lookup_string[2], (FRESH_ITEMS_ALL, SSM_HEADS), jnp.float32, math.log(0.5), math.log(2.0)))
    spurt_spans = jax.random.uniform(lookup_string[3], (FRESH_ITEMS_ALL,), jnp.float32) < 3.0 / SHARD_FRESH_ITEMS
    grand_quantity = jax.random.uniform(lookup_string[4], (FRESH_ITEMS_ALL,), jnp.float32, 0.22, 0.69)
    concluding_result = -(forgetting_speeds[query_group] * multiplier_value[query_group][:, None] * approximate_guess) - jnp.where(spurt_spans, grand_quantity, 0.0)[:, None]
    return concluding_result.astype(jnp.float32)


def plant(result, rng, low, largest):
    longest = result.shape.index(max(result.shape))
    spots = []
    for shift in (0, 1):
        where = [jax.random.randint(jax.random.fold_in(rng, axis), (), 0, length) for axis, length in enumerate(result.shape)]
        where[longest] = (where[longest] + shift) % result.shape[longest]
        spots.append(tuple(where))
    return result.at[spots[0]].set(low).at[spots[1]].set(largest)


def block_scale(stream_key, extent, cuts, smallest, high):
    factor_of = 1.0
    for axis_at, parts in cuts:
        steps = jax.random.uniform(jax.random.fold_in(jax.random.fold_in(stream_key, 6), axis_at), (parts,), jnp.float32, smallest / len(cuts), high / len(cuts))
        factor_of = factor_of * jnp.repeat(jnp.exp(steps), extent[axis_at] // parts).reshape((-1,) + (1,) * (len(extent) - 1 - axis_at))
    return factor_of


def deal_out(stream_key, own, number, rows, number_of, top, limit, skew):
    sequence = jax.random.permutation(stream_key, number_of)
    heavy_load, ordinary = load_shares(number_of, rows * top, limit, skew, True), load_shares(number_of, rows * top, limit, skew, False)
    places = jnp.arange(number_of)

    def named(tallies, offset_by):
        used = int((tallies > 0).sum())
        fixed = max(1, used // 4)
        moved = fixed + (places - fixed + offset_by * (used - fixed)) % max(1, number_of - fixed)
        return jnp.zeros((number_of,), jnp.int32).at[sequence[jnp.where(places < fixed, places, moved)]].set(jnp.asarray(tallies, jnp.int32))

    tallies = jnp.where(number % 4 == 0, named(heavy_load, number // 4), named(ordinary, number - number // 4 - 1))
    mixed = jax.random.permutation(jax.random.fold_in(own, 3), number_of)
    giver, taker = mixed[0:number_of // 2 * 2:2], mixed[1:number_of // 2 * 2:2]
    slack = jnp.minimum(tallies[giver] - 1, limit - tallies[taker]) // 2
    slack = jnp.where((giver == sequence[0]) | (taker == sequence[0]) | (tallies[taker] == 0), 0, jnp.maximum(slack, 0))
    moved = jax.random.randint(jax.random.fold_in(own, 4), (number_of // 2,), 0, 1 << 20) % (slack + 1)
    tallies = tallies.at[giver].add(-moved).at[taker].add(moved)
    items = jnp.searchsorted(jnp.cumsum(tallies), jnp.arange(rows * top), side="right").astype(jnp.int32)
    grid = items.reshape(top, rows).T
    grid = grid[jax.random.permutation(jax.random.fold_in(own, 1), rows)]
    offset_by = jax.random.randint(jax.random.fold_in(own, 2), (rows, 1), 0, top)
    return jnp.take_along_axis(grid, (jnp.arange(top)[None, :] + offset_by) % top, axis=1)


def load_shares(number_of, total, bound, lean, full):
    portions = [(1 << 20) // math.isqrt(standing ** lean) + 1 for standing in range(1, number_of + 1)]
    largest = bound if full else min(bound, max(-(-total // number_of), total * portions[0] // sum(portions)))
    least = 1 if total - largest >= number_of - 1 else 0
    given, surplus = [largest] + [least] * (number_of - 1), total - largest - least * (number_of - 1)
    while surplus > 0:
        movable = [i for i in range(1, number_of) if given[i] < largest] or [i for i in range(1, number_of) if given[i] < bound]
        pool, remaining = sum([portions[i] for i in movable]), surplus
        for i in movable:
            extra = min(bound - given[i], max(1, remaining * portions[i] // pool), surplus)
            given[i] = given[i] + extra
            surplus = surplus - extra
    return np.array(given)


def centred(stream_key, extent, scale, bound, pieces=(), held_as=jnp.bfloat16):
    result = jax.random.normal(stream_key, extent, jnp.float32) * scale
    if len(pieces) > 0:
        result = block_scale(stream_key, extent, pieces, -0.22, 0.18) * result
    return jnp.clip(result, min=-bound, max=bound).astype(held_as)


def setup_inputs(seed: int = 0) -> dict:
    key_list = jax.random.split(jax.random.key(seed), 20)
    tokens = centred(key_list[0], (FRESH_ITEMS_ALL, D), 1.0, 6.0, ((0, 32),))
    queries = draw_queries(jax.random.fold_in(key_list[19], 71), 0)
    keys_values = draw_keys_values(jax.random.fold_in(key_list[19], 71), 0)
    scan_input = centred(key_list[3], (FRESH_ITEMS_ALL, SSM_HEADS * SSM_DIM), 1.0, 6.0, ((0, 32),))
    state_maps = centred(key_list[4], (FRESH_ITEMS_ALL, 2 * NSTATE), 0.25, 1.5, ((0, 32),), jnp.float32)
    step_size = jnp.clip(jnp.exp(math.log(0.5) - 2.3025851 * jax.random.uniform(key_list[5], (FRESH_ITEMS_ALL, SSM_HEADS), jnp.float32) ** block_scale(key_list[5], (FRESH_ITEMS_ALL, SSM_HEADS), ((0, 32),), -0.2, 0.2)), 0.05, 0.5)
    step_decay = draw_step_decay(jax.random.fold_in(key_list[19], 71), 0)
    block_pool = centred(key_list[7], (POOL * DEVICES, BLOCK, 2 * KV_HEADS * HEAD), 1.0, 5.0, ((0, 32),))
    state_pool = centred(key_list[8], (SPOOL * DEVICES, SSM_HEADS * SSM_DIM * NSTATE), 1.0, 5.0, ((0, 32),), jnp.float32)
    block_holder = draw_block_holder(jax.random.fold_in(key_list[19], 71), 0)
    block_index = plant(jax.random.randint(key_list[10], (REQS, MAXB), 0, POOL), jax.random.fold_in(key_list[10], 1), 0, POOL - 1).astype(jnp.int32)
    cached_blocks = draw_cached_blocks(jax.random.fold_in(key_list[19], 71), 0)
    state_holder = plant(jax.random.randint(key_list[12], (REQS,), 0, N_DP), jax.random.fold_in(key_list[12], 1), 0, N_DP - 1).astype(jnp.int32)
    state_index = plant(jax.random.randint(key_list[13], (REQS,), 0, SPOOL), jax.random.fold_in(key_list[13], 1), 0, SPOOL - 1).astype(jnp.int32)
    norm_gain = jnp.clip(1.0 + 0.18 * jax.random.normal(key_list[14], (D,), jnp.float32), 0.1, 1.9)
    router_weight = centred(key_list[15], (D, EXPERTS), D ** -0.5, 0.09375)
    expert_ids_keys = jax.random.split(jax.random.fold_in(key_list[16], 1), FRESH_ITEMS_ALL // SHARD_FRESH_ITEMS)
    expert_ids_turns = jax.random.permutation(jax.random.fold_in(key_list[16], 3), FRESH_ITEMS_ALL // SHARD_FRESH_ITEMS)
    expert_ids = jax.vmap(lambda own, number: deal_out(jax.random.fold_in(key_list[16], 2), own, number, SHARD_FRESH_ITEMS, EXPERTS, 2, CAP, 0))(expert_ids_keys, expert_ids_turns).reshape((FRESH_ITEMS_ALL, 2))
    up_weight = centred(key_list[17], (EXPERTS, D, FF), D ** -0.5, 0.09375, ((0, 8), (2, 4)))
    down_weight = centred(key_list[18], (EXPERTS, FF, D), FF ** -0.5, 0.0625, ((0, 8), (1, 4)))
    return dict(tokens=tokens, queries=queries, keys_values=keys_values, scan_input=scan_input, state_maps=state_maps, step_size=step_size, step_decay=step_decay, block_pool=block_pool, state_pool=state_pool, block_holder=block_holder, block_index=block_index, cached_blocks=cached_blocks, state_holder=state_holder, state_index=state_index, norm_gain=norm_gain, router_weight=router_weight, expert_ids=expert_ids, up_weight=up_weight, down_weight=down_weight)


def attend(queries, keys_values, prefix, cached_count):
    length = queries.shape[0]
    groups = HEADS // KV_HEADS
    past_len = prefix.shape[0] * prefix.shape[1]
    joined = jnp.concatenate([prefix.reshape(past_len, -1), keys_values], 0)
    joined = joined.astype(jnp.float32).reshape(past_len + length, 2, KV_HEADS, HEAD)
    key_rows = joined[:, 0]
    values = joined[:, 1]
    grouped = queries.astype(jnp.float32).reshape(length, KV_HEADS, groups, HEAD)
    scores = jnp.einsum('tgqd,kgd->gqtk', grouped, key_rows, precision=lax.Precision.HIGHEST) * HEAD ** (-0.5)
    places = jnp.arange(past_len + length, dtype=jnp.int32)
    tokens_at = jnp.arange(length, dtype=jnp.int32)
    visible = jnp.where(places[None, :] < past_len, places[None, :] < cached_count * BLOCK, places[None, :] - past_len <= tokens_at[:, None])
    scores = jnp.where(visible, scores, -jnp.inf)
    row_max = lax.optimization_barrier(jnp.max(scores, axis=-1, keepdims=True))
    weights = jnp.exp(scores - row_max)
    weights = lax.optimization_barrier((weights / lax.optimization_barrier(jnp.sum(weights, axis=-1, keepdims=True))).astype(jnp.bfloat16))
    output = jnp.einsum('gqtk,kgd->tgqd', weights.astype(jnp.float32), values, precision=lax.Precision.HIGHEST)
    return output.reshape(length, -1)

def state_block(inputs, state_maps, steps, decays, start_flat):
    length = inputs.shape[0]
    values = inputs.astype(jnp.float32).reshape(length, SSM_HEADS, SSM_DIM)
    entry_maps = state_maps[:, :NSTATE]
    readout = state_maps[:, NSTATE:]
    running = jnp.cumsum(decays, axis=0)
    places = jnp.arange(length, dtype=jnp.int32)
    causal = (places[:, None] >= places[None, :])[:, :, None]
    spread = running[:, None, :] - running[None, :, :]
    fading = jnp.where(causal, jnp.exp(jnp.where(causal, spread, 0.0)), 0.0)
    intersection = jnp.dot(readout, entry_maps.T, precision=lax.Precision.HIGHEST)
    mixing = fading * intersection[:, :, None] * steps[None, :, :]
    output = jnp.einsum('tsh,shp->thp', mixing, values, precision=lax.Precision.HIGHEST)
    start_state = start_flat.reshape(SSM_HEADS, SSM_DIM, NSTATE)
    output = output + jnp.exp(running)[:, :, None] * jnp.einsum('tn,hpn->thp', readout, start_state, precision=lax.Precision.HIGHEST)
    last_sum = running[-1]
    weight = jnp.exp(last_sum[None, :] - running) * steps
    final_state = jnp.exp(last_sum)[:, None, None] * start_state + jnp.einsum('sh,shp,sn->hpn', weight, values, entry_maps, precision=lax.Precision.HIGHEST)
    return (output.reshape(length, -1), final_state.reshape(-1))

def one_request(request_items):
    queries, keys_values, inputs, state_maps, steps, decays, prefix, cached_count, start_flat = request_items
    attended = attend(queries, keys_values, prefix, cached_count)
    ssm_out, final_state = state_block(inputs, state_maps, steps, decays, start_flat)
    return (attended + ssm_out, final_state)

def by_request(array):
    return array.reshape((REQS, SHARD_FRESH_ITEMS) + array.shape[1:])

def reference(tokens, queries, keys_values, scan_input, state_maps, step_size, step_decay, block_pool, state_pool, block_holder, block_index, cached_blocks, state_holder, state_index, norm_gain, router_weight, expert_ids, up_weight, down_weight):
    column = jnp.arange(REQS, dtype=jnp.int32) % N_EXPERT
    usable = jnp.arange(MAXB, dtype=jnp.int32)[None, :] < cached_blocks[:, None]
    block_rows = (block_holder * N_EXPERT + column[:, None]) * POOL + block_index
    block_rows = jnp.where(usable, block_rows, 0).astype(jnp.int32)
    prefix = block_pool[block_rows]
    state_rows = ((state_holder * N_EXPERT + column) * SPOOL + state_index).astype(jnp.int32)
    starting = state_pool[state_rows]
    mixers, final_state = lax.map(one_request, (by_request(queries), by_request(keys_values), by_request(scan_input), by_request(state_maps), by_request(step_size), by_request(step_decay), prefix, cached_blocks, starting))
    mixed_rows = (tokens.astype(jnp.float32) + mixers.reshape(FRESH_ITEMS_ALL, D)).astype(jnp.bfloat16)
    mixed_wide = lax.optimization_barrier(mixed_rows).astype(jnp.float32)
    normed = (mixed_wide * lax.rsqrt(lax.optimization_barrier(jnp.mean(mixed_wide * mixed_wide, axis=-1, keepdims=True)) + 1e-05) * norm_gain).astype(jnp.bfloat16)
    logits = jnp.dot(normed, router_weight, preferred_element_type=jnp.float32)
    chosen = jnp.take_along_axis(logits, expert_ids, axis=1)
    lifted = jax.nn.sigmoid(chosen)
    gate_values = lifted / lax.optimization_barrier(jnp.sum(lifted, axis=1, keepdims=True))
    expert_list = expert_ids.reshape(DEVICES, 2 * SHARD_FRESH_ITEMS)
    onehot = (expert_list[:, :, None] == jnp.arange(EXPERTS, dtype=jnp.int32)[None, None, :]).astype(jnp.int32)
    before = jnp.cumsum(onehot, axis=1) - onehot
    slot_ids = lax.optimization_barrier(jnp.sum(before * onehot, axis=2))
    target = (expert_list * CAP + slot_ids).astype(jnp.int32)
    owner_ids = jnp.arange(2 * SHARD_FRESH_ITEMS, dtype=jnp.int32) // 2
    source = lax.optimization_barrier(jnp.sum(jnp.where(target[:, :, None] == jnp.arange(EXPERTS * CAP, dtype=jnp.int32)[None, None, :], owner_ids[None, :, None], 0), axis=1))
    source = source + jnp.arange(DEVICES, dtype=jnp.int32)[:, None] * SHARD_FRESH_ITEMS
    by_expert = source.reshape(DEVICES, EXPERTS, CAP).transpose(1, 0, 2).reshape(EXPERTS, DEVICES * CAP).astype(jnp.int32)

    def one_expert(expert_items):
        row_ids, upper_full, lower_full = expert_items
        gathered = normed[row_ids]
        upper = upper_full.reshape(D, N_DP, FF_DEV)
        lower = lower_full.reshape(N_DP, FF_DEV, D)
        totals = jnp.zeros((DEVICES * CAP, D), jnp.float32)
        for shard in range(N_DP):
            hidden = jax.nn.silu(jnp.dot(gathered, upper[:, shard], preferred_element_type=jnp.float32)).astype(jnp.bfloat16)
            partial_value = lax.optimization_barrier(jnp.dot(hidden, lower[shard], preferred_element_type=jnp.float32).astype(jnp.bfloat16))
            totals = totals + partial_value.astype(jnp.float32)
        return totals
    sums = lax.map(one_expert, (by_expert, up_weight, down_weight))
    sums = sums.reshape(EXPERTS, DEVICES, CAP, D).transpose(1, 0, 2, 3).reshape(DEVICES, EXPERTS * CAP, D)
    picked = jnp.take_along_axis(sums, target[:, :, None], axis=1)
    combined = lax.optimization_barrier(jnp.sum(picked.reshape(FRESH_ITEMS_ALL, 2, D) * gate_values[:, :, None], axis=1))
    layer_out = (mixed_wide + combined).astype(jnp.bfloat16)
    return (layer_out, final_state)
```

```python
import functools

import jax
import jax.numpy as jnp
from jax import lax
from jax.experimental import pallas as pl
from jax.experimental.pallas import tpu as pltpu
from jax.sharding import PartitionSpec as P

HEADS = 32
KV_HEADS = 8
HEAD = 128
SSM_HEADS = 64
SSM_DIM = 64
NSTATE = 16
BLOCK = 16
LANES = 128
HIGH = lax.Precision.HIGHEST
F32 = jnp.float32
BF16 = jnp.bfloat16
VMEM = pl.BlockSpec(memory_space=pltpu.VMEM)
SMEM = pl.BlockSpec(memory_space=pltpu.SMEM)


def split_rows(value):
    high = value.astype(BF16)
    low = (value - high.astype(F32)).astype(BF16)
    return jnp.concatenate([high, low], 0)


def spread(column_pair, width):
    rows = column_pair.shape[0]
    lane = lax.broadcasted_iota(jnp.int32, (rows, LANES), 1)
    return jnp.where(
        lane < width,
        jnp.broadcast_to(column_pair[:, 0:1], (rows, LANES)),
        jnp.broadcast_to(column_pair[:, 1:2], (rows, LANES)),
    )


def pack_kernel(slot, *refs):
    asked_ref = refs[0]
    blocks = refs[1 : 1 + slot]
    state_ref = refs[1 + slot]
    out_ref = refs[2 + slot]
    for s in range(slot):
        out_ref[0, s * BLOCK : (s + 1) * BLOCK, :] = blocks[s][0]
    base = slot * BLOCK
    width = out_ref.shape[2]
    groups = width // LANES
    rows = state_ref.shape[1] // groups
    for b in range(groups):
        out_ref[0, base : base + rows, b * LANES : (b + 1) * LANES] = state_ref[
            0, b * rows : (b + 1) * rows, :
        ]


def pack(asked, block_pool, states):
    peers = asked.shape[0]
    slot = asked.shape[1] - 1
    width = block_pool.shape[2]
    state_rows = states.shape[1] * LANES // width
    rows = slot * BLOCK + state_rows

    def block_spec(s):
        return pl.BlockSpec((1, BLOCK, width), lambda j, asked_ref: (asked_ref[j, s], 0, 0))

    return pl.pallas_call(
        functools.partial(pack_kernel, slot),
        out_shape=jax.ShapeDtypeStruct((peers, rows, width), BF16),
        grid_spec=pltpu.PrefetchScalarGridSpec(
            num_scalar_prefetch=1,
            grid=(peers,),
            in_specs=[block_spec(s) for s in range(slot)]
            + [pl.BlockSpec((1,) + states.shape[1:], lambda j, asked_ref: (asked_ref[j, slot], 0, 0))],
            out_specs=pl.BlockSpec((1, rows, width), lambda j, asked_ref: (j, 0, 0)),
        ),
        name="pack",
    )(asked, *([block_pool] * slot), states)


def scan_kernel(x_ref, maps_ref, steps_ref, decays_ref, tokens_ref, sum_ref, local_ref, fade_ref, keep_ref):
    length = x_ref.shape[0]
    rows_i = lax.broadcasted_iota(jnp.int32, (length, length), 0)
    cols_i = lax.broadcasted_iota(jnp.int32, (length, length), 1)
    causal = rows_i >= cols_i
    running = jnp.dot(
        causal.astype(F32), decays_ref[...], precision=HIGH, preferred_element_type=F32
    )
    last = running[length - 1 : length, :]
    middle = 0.5 * last
    rise = jnp.exp(running - middle)
    fall = jnp.exp(middle - running) * steps_ref[...]
    half = jnp.exp(middle)
    fade_ref[...] = jnp.exp(running)
    keep_ref[...] = jnp.exp(last)
    entry = maps_ref[:, :NSTATE]
    readout = maps_ref[:, NSTATE:]
    meeting = lax.dot_general(
        readout, entry, (((1,), (1,)), ((), ())), precision=HIGH, preferred_element_type=F32
    )
    meeting = split_rows(jnp.where(causal, meeting, 0.0))
    per = LANES // NSTATE
    tiled = jnp.concatenate([entry] * per, 1)
    tiled_high = tiled.astype(BF16)
    tiled_low = (tiled - tiled_high.astype(F32)).astype(BF16)
    tiled = jnp.concatenate([tiled_high, tiled_low], 1)
    sub = lax.broadcasted_iota(jnp.int32, (LANES, LANES), 0)
    lane = lax.broadcasted_iota(jnp.int32, (LANES, LANES), 1)
    own = (sub % per) == (lane // NSTATE)
    heads_per = LANES // SSM_DIM
    state_rows = LANES // per
    for q in range(x_ref.shape[1] // LANES):
        cols = slice(q * LANES, (q + 1) * LANES)
        pair = slice(q * heads_per, (q + 1) * heads_per)
        drive = (x_ref[:, cols].astype(F32) * spread(fall[:, pair], SSM_DIM)).astype(BF16)
        both = jnp.dot(meeting, drive, preferred_element_type=F32)
        part = both[:length] + both[length:]
        sum_ref[:, cols] = tokens_ref[:, cols].astype(F32) + part * spread(rise[:, pair], SSM_DIM)
        outer = lax.dot_general(
            drive, tiled, (((0,), (0,)), ((), ())), preferred_element_type=F32
        )
        outer = jnp.where(own, outer[:, :LANES] + outer[:, LANES:], 0.0)
        folded = jnp.sum(outer.reshape(state_rows, per, LANES), axis=1)
        upper = lax.broadcasted_iota(jnp.int32, (state_rows, LANES), 0) < state_rows // 2
        scale = jnp.where(
            upper,
            jnp.broadcast_to(half[:, q * heads_per : q * heads_per + 1], (state_rows, LANES)),
            jnp.broadcast_to(half[:, q * heads_per + 1 : q * heads_per + 2], (state_rows, LANES)),
        )
        local_ref[q * state_rows : (q + 1) * state_rows, :] = folded * scale


def scan_local(x, maps, steps, decays, tokens):
    length, width = x.shape
    return pl.pallas_call(
        scan_kernel,
        out_shape=(
            jax.ShapeDtypeStruct((length, width), F32),
            jax.ShapeDtypeStruct((width * NSTATE // LANES, LANES), F32),
            jax.ShapeDtypeStruct(steps.shape, F32),
            jax.ShapeDtypeStruct((1, steps.shape[1]), F32),
        ),
        in_specs=[VMEM] * 5,
        out_specs=(VMEM,) * 4,
        name="scan_local",
    )(x, maps, steps, decays, tokens)


def mix_kernel(
    owner_ref,
    q_ref,
    kv_ref,
    got_ref,
    known_ref,
    sum_ref,
    local_ref,
    fade_ref,
    keep_ref,
    maps_ref,
    gain_ref,
    pick_ref,
    mixed_ref,
    normed_ref,
    send_ref,
    final_ref,
    total_ref,
):
    length, width = q_ref.shape
    peers = got_ref.shape[0]
    groups = HEADS // KV_HEADS
    state_rows = width * NSTATE // kv_ref.shape[1]
    block_rows = got_ref.shape[1] - state_rows
    past = peers * block_rows
    owner = owner_ref[0]
    per = LANES // NSTATE
    fold = LANES // per
    heads_per = LANES // SSM_DIM
    readout = maps_ref[:, NSTATE:]
    readout = split_rows(jnp.concatenate([readout] * per, 1))
    sub = lax.broadcasted_iota(jnp.int32, (fold, per, LANES), 1)
    lane = lax.broadcasted_iota(jnp.int32, (fold, per, LANES), 2)
    own = sub == lane // NSTATE
    fade = fade_ref[...]
    keep = keep_ref[...]
    token = lax.broadcasted_iota(jnp.int32, (length, length), 0)
    other = lax.broadcasted_iota(jnp.int32, (length, length), 1)
    seen = jnp.concatenate(
        [
            jnp.broadcast_to(known_ref[...], (length, past)),
            jnp.where(other <= token, 0.0, -1e30).astype(F32),
        ],
        1,
    )
    seen = jnp.concatenate([seen] * groups, 0)
    half = kv_ref.shape[1] // 2
    squares = jnp.zeros((length, LANES), F32)
    for g in range(KV_HEADS):
        key_cols = slice(g * HEAD, (g + 1) * HEAD)
        value_cols = slice(half + g * HEAD, half + (g + 1) * HEAD)
        keys = jnp.concatenate(
            [got_ref[j, 0:block_rows, key_cols] for j in range(peers)] + [kv_ref[:, key_cols]], 0
        )
        values = jnp.concatenate(
            [got_ref[j, 0:block_rows, value_cols] for j in range(peers)] + [kv_ref[:, value_cols]], 0
        )
        asks = jnp.concatenate(
            [
                q_ref[:, (g * groups + i) * HEAD : (g * groups + i + 1) * HEAD]
                for i in range(groups)
            ],
            0,
        )
        scores = (
            lax.dot_general(asks, keys, (((1,), (1,)), ((), ())), preferred_element_type=F32)
            * HEAD ** (-0.5)
            + seen
        )
        top = jnp.max(scores, axis=1, keepdims=True)
        weights = jnp.exp(scores - top)
        weights = (weights * (1.0 / jnp.sum(weights, axis=1, keepdims=True))).astype(BF16)
        attended = jnp.dot(weights, values, preferred_element_type=F32)
        for i in range(groups):
            q = g * groups + i
            cols = slice(q * LANES, (q + 1) * LANES)
            per_side = state_rows // fold
            rows_at = block_rows + (q % per_side) * fold
            start = got_ref[
                owner, rows_at : rows_at + fold, (q // per_side) * LANES : (q // per_side + 1) * LANES
            ].astype(F32)
            wide = jnp.where(own, jnp.broadcast_to(start[:, None, :], (fold, per, LANES)), 0.0)
            wide = wide.reshape(LANES, LANES).astype(BF16)
            both = lax.dot_general(
                readout, wide, (((1,), (1,)), ((), ())), preferred_element_type=F32
            )
            pair = slice(q * heads_per, (q + 1) * heads_per)
            carried = (both[:length] + both[length:]) * spread(fade[:, pair], SSM_DIM)
            upper = lax.broadcasted_iota(jnp.int32, (fold, LANES), 0) < fold // 2
            scale = jnp.where(
                upper,
                jnp.broadcast_to(keep[:, q * heads_per : q * heads_per + 1], (fold, LANES)),
                jnp.broadcast_to(keep[:, q * heads_per + 1 : q * heads_per + 2], (fold, LANES)),
            )
            final_ref[q * fold : (q + 1) * fold, :] = (
                scale * start + local_ref[q * fold : (q + 1) * fold, :]
            )
            mixed = (sum_ref[:, cols] + attended[i * length : (i + 1) * length] + carried).astype(BF16)
            mixed_ref[:, cols] = mixed
            mixed = mixed.astype(F32)
            total_ref[:, cols] = mixed
            squares = squares + mixed * mixed
    mean = jnp.sum(squares, axis=1, keepdims=True) * (1.0 / width)
    scale = lax.rsqrt(mean + 1e-05)
    step = 4 * LANES
    for q in range(width // step):
        cols = slice(q * step, (q + 1) * step)
        normed = (total_ref[:, cols] * scale * gain_ref[:, cols]).astype(BF16)
        normed_ref[:, cols] = normed
        rows = jnp.dot(pick_ref[...], normed, preferred_element_type=F32).astype(BF16)
        for i in range(send_ref.shape[0]):
            send_ref[i, :, cols] = rows


def mix(owner, queries, keys_values, got, known, sums, local, fade, keep, maps, gain, pick, copies):
    length, width = queries.shape
    return pl.pallas_call(
        mix_kernel,
        out_shape=(
            jax.ShapeDtypeStruct((length, width), BF16),
            jax.ShapeDtypeStruct((length, width), BF16),
            jax.ShapeDtypeStruct((copies, pick.shape[0], width), BF16),
            jax.ShapeDtypeStruct(local.shape, F32),
        ),
        in_specs=[SMEM] + [VMEM] * 11,
        out_specs=(VMEM,) * 4,
        scratch_shapes=[pltpu.VMEM((length, width), F32)],
        name="mix",
    )(owner, queries, keys_values, got, known, sums, local, fade, keep, maps, gain, pick)


def choose_kernel(rows_ref, pick_ref, send_ref):
    step = 4 * LANES
    for q in range(rows_ref.shape[1] // step):
        cols = slice(q * step, (q + 1) * step)
        rows = jnp.dot(pick_ref[...], rows_ref[:, cols], preferred_element_type=F32).astype(BF16)
        for i in range(send_ref.shape[0]):
            send_ref[i, :, cols] = rows


def choose(rows, pick, copies):
    return pl.pallas_call(
        choose_kernel,
        out_shape=jax.ShapeDtypeStruct((copies, pick.shape[0], rows.shape[1]), BF16),
        in_specs=[VMEM] * 2,
        out_specs=VMEM,
        name="choose",
    )(rows, pick)


def combine_kernel(parts_ref, weights_ref, out_ref):
    length = out_ref.shape[0]
    both = jnp.dot(weights_ref[...], parts_ref[...], preferred_element_type=F32)
    out_ref[...] = (both[:length] + both[length:]).astype(out_ref.dtype)


def combine(parts, weights, dtype):
    rows, width = parts.shape
    length = weights.shape[0] // 2
    step = 8 * LANES
    return pl.pallas_call(
        combine_kernel,
        out_shape=jax.ShapeDtypeStruct((length, width), dtype),
        grid=(width // step,),
        in_specs=[
            pl.BlockSpec((rows, step), lambda i: (0, i)),
            pl.BlockSpec(weights.shape, lambda i: (0, 0)),
        ],
        out_specs=pl.BlockSpec((length, step), lambda i: (0, i)),
        name="combine",
    )(parts, weights)


def finish_kernel(parts_ref, weights_ref, mixed_ref, far_ref, out_ref):
    length = out_ref.shape[0]
    both = jnp.dot(weights_ref[...], parts_ref[...], preferred_element_type=F32)
    summed = both[:length] + both[length:] + far_ref[...].astype(F32)
    out_ref[...] = (mixed_ref[...].astype(F32) + summed).astype(out_ref.dtype)


def finish(parts, weights, mixed, far):
    rows, width = parts.shape
    length = weights.shape[0] // 2
    step = 8 * LANES
    narrow = pl.BlockSpec((length, step), lambda i: (0, i))
    return pl.pallas_call(
        finish_kernel,
        out_shape=jax.ShapeDtypeStruct((length, width), BF16),
        grid=(width // step,),
        in_specs=[
            pl.BlockSpec((rows, step), lambda i: (0, i)),
            pl.BlockSpec(weights.shape, lambda i: (0, 0)),
            narrow,
            narrow,
        ],
        out_specs=narrow,
        name="finish",
    )(parts, weights, mixed, far)


def targets(expert_list, experts):
    capacity = expert_list.shape[0] // experts
    onehot = (expert_list[:, None] == jnp.arange(experts, dtype=jnp.int32)[None, :]).astype(F32)
    number = expert_list.shape[0]
    places = jnp.arange(number, dtype=jnp.int32)
    earlier = (places[:, None] > places[None, :]).astype(F32)
    before = jnp.dot(earlier, onehot, preferred_element_type=F32)
    slot = jnp.sum(before * onehot, axis=1).astype(jnp.int32)
    return expert_list * capacity + slot


def one_hots(expert_list, experts):
    target = targets(expert_list, experts).reshape(-1, 2)
    places = jnp.arange(expert_list.shape[0], dtype=jnp.int32)
    return target[:, :, None] == places[None, None, :]


def picker(hot):
    return jnp.any(hot, axis=1).T.astype(BF16)


def gate_weights(rows, router_weight, expert_ids, hot, copies):
    logits = jnp.dot(rows, router_weight, preferred_element_type=F32)
    named = expert_ids[:, :, None] == jnp.arange(router_weight.shape[1], dtype=jnp.int32)
    chosen = jnp.sum(jnp.where(named, logits[:, None, :], 0.0), axis=2)
    lifted = jax.nn.sigmoid(chosen)
    gates = lifted / jnp.sum(lifted, axis=1, keepdims=True)
    weights = jnp.sum(jnp.where(hot, gates[:, :, None], 0.0), axis=1)
    weights = jnp.concatenate([weights] * copies, 1)
    return split_rows(weights)


def apply_expert(rows, up_local, down_local):
    hidden = jax.nn.silu(jnp.dot(rows, up_local, preferred_element_type=F32)).astype(BF16)
    return jnp.dot(hidden, down_local, preferred_element_type=F32).astype(BF16)


def local(
    tokens,
    queries,
    keys_values,
    scan_input,
    state_maps,
    step_size,
    step_decay,
    block_pool,
    state_pool,
    block_holder,
    block_index,
    cached_blocks,
    state_holder,
    state_index,
    norm_gain,
    router_weight,
    expert_ids,
    up_weight,
    down_weight,
):
    peers = lax.axis_size("dp")
    columns = lax.axis_size("expert")
    near = peers // 2
    ring = [(k, (k + near) % peers) for k in range(peers)]
    groups = [
        [(h * near + i) * columns + c for i in range(near) for c in range(columns)]
        for h in range(2)
    ]
    experts = router_weight.shape[1]
    holders = block_holder[0]
    indices = block_index[0]
    entries = holders.shape[0]
    slot = entries // peers

    def swap(rows):
        return lax.all_to_all(
            rows,
            ("dp", "expert"),
            split_axis=0,
            concat_axis=0,
            tiled=True,
            axis_index_groups=groups,
        )

    places = jnp.arange(entries, dtype=jnp.int32)
    same = holders[:, None] == holders[None, :]
    rank = jnp.sum((same & (places[None, :] < places[:, None])).astype(jnp.int32), axis=1)
    seat = holders * slot + rank
    at_seat = seat[None, :] == places[:, None]
    wanted = jnp.sum(jnp.where(at_seat, indices[None, :], 0), axis=1)
    entry = jnp.sum(jnp.where(at_seat, places[None, :], 0), axis=1)
    known = jnp.where(entry < cached_blocks[0], 0.0, -1e30).astype(F32)
    known = jnp.repeat(known, BLOCK)[None, :]
    state_wanted = jnp.broadcast_to(state_index[0], (peers, 1))
    mine = expert_ids.reshape(-1)
    ask = jnp.concatenate(
        [
            wanted.reshape(peers, slot),
            state_wanted,
            jnp.broadcast_to(mine[None], (peers, mine.shape[0])),
        ],
        1,
    )
    asked = lax.all_to_all(ask, "dp", split_axis=0, concat_axis=0, tiled=True)
    partner = (lax.axis_index("dp") + near) % peers
    theirs = lax.dynamic_index_in_dim(asked[:, slot + 1 :], partner, 0, keepdims=False)

    states = state_pool.reshape(state_pool.shape[0], -1, LANES).astype(BF16)
    packed = pack(asked[:, : slot + 1], block_pool, states)
    got = lax.all_to_all(packed, "dp", split_axis=0, concat_axis=0, tiled=True)

    hot = one_hots(mine, experts)
    pick = picker(hot)
    sums, from_inputs, fade, keep = scan_local(
        scan_input, state_maps, step_size, step_decay, tokens
    )
    mixed, normed, send, final_state = mix(
        state_holder,
        queries,
        keys_values,
        got,
        known,
        sums,
        from_inputs,
        fade,
        keep,
        state_maps,
        norm_gain[None, :],
        pick,
        near,
    )
    capacity = mine.shape[0] // experts
    width = tokens.shape[1]
    up_local = up_weight[0]
    down_local = down_weight[0]

    far_rows = lax.ppermute(normed, "dp", ring)
    near_in = swap(send.reshape(near * experts, capacity, width))
    far_hot = one_hots(theirs, experts)
    far_send = choose(far_rows, picker(far_hot), near)
    far_in = swap(far_send.reshape(near * experts, capacity, width))

    near_out = apply_expert(near_in.reshape(-1, width), up_local, down_local)
    far_out = apply_expert(far_in.reshape(-1, width), up_local, down_local)
    near_weights = gate_weights(normed, router_weight, expert_ids, hot, near)
    far_weights = gate_weights(
        far_rows, router_weight, theirs.reshape(expert_ids.shape), far_hot, near
    )
    far_back = swap(far_out.reshape(near_in.shape)).reshape(-1, width)
    far_sum = lax.ppermute(combine(far_back, far_weights, BF16), "dp", ring)
    near_back = swap(near_out.reshape(near_in.shape)).reshape(-1, width)
    layer_out = finish(near_back, near_weights, mixed, far_sum)
    return (layer_out, final_state.reshape(1, -1))


def solution(mesh):
    placed = (
        P(("dp", "expert"), None),
        P(("dp", "expert"), None),
        P(("dp", "expert"), None),
        P(("dp", "expert"), None),
        P(("dp", "expert"), None),
        P(("dp", "expert"), None),
        P(("dp", "expert"), None),
        P(("dp", "expert"), None, None),
        P(("dp", "expert"), None),
        P(("dp", "expert"), None),
        P(("dp", "expert"), None),
        P(("dp", "expert")),
        P(("dp", "expert")),
        P(("dp", "expert")),
        P(),
        P(),
        P(("dp", "expert"), None),
        P("expert", None, "dp"),
        P("expert", "dp", None),
    )
    return jax.shard_map(
        local,
        mesh=mesh,
        in_specs=placed,
        out_specs=(P(("dp", "expert"), None), P(("dp", "expert"), None)),
        check_vma=False,
    )
```

```python
import functools

import jax
import jax.numpy as jnp
from jax import lax
from jax.experimental import pallas as pl
from jax.experimental.pallas import tpu as pltpu
from jax.sharding import PartitionSpec as P


HEADS = 32
KV_HEADS = 8
HEAD = 128
SSM_DIM = 64
NSTATE = 16
BLOCK = 16
LANES = 128
HIGH = lax.Precision.HIGHEST
F32 = jnp.float32
BF16 = jnp.bfloat16
VMEM = pl.BlockSpec(memory_space=pltpu.VMEM)
SMEM = pl.BlockSpec(memory_space=pltpu.SMEM)


def split_rows(value):
    high = value.astype(BF16)
    low = (value - high.astype(F32)).astype(BF16)
    return jnp.concatenate([high, low], 0)


def spread(column_pair, width):
    rows = column_pair.shape[0]
    lane = lax.broadcasted_iota(jnp.int32, (rows, LANES), 1)
    return jnp.where(
        lane < width,
        jnp.broadcast_to(column_pair[:, 0:1], (rows, LANES)),
        jnp.broadcast_to(column_pair[:, 1:2], (rows, LANES)),
    )


def pack_kernel(slot, *refs):
    blocks = refs[1 : 1 + slot]
    state_ref = refs[1 + slot]
    out_ref = refs[2 + slot]
    for s in range(slot):
        out_ref[0, s * BLOCK : (s + 1) * BLOCK, :] = blocks[s][0]
    base = slot * BLOCK
    width = out_ref.shape[2]
    groups = width // LANES
    rows = state_ref.shape[1] // groups
    for b in range(groups):
        out_ref[0, base : base + rows, b * LANES : (b + 1) * LANES] = state_ref[
            0, b * rows : (b + 1) * rows, :
        ]


def pack(asked, block_pool, states):
    peers = asked.shape[0]
    slot = asked.shape[1] - 1
    width = block_pool.shape[2]
    state_rows = states.shape[1] * LANES // width
    rows = slot * BLOCK + state_rows

    def block_spec(s):
        return pl.BlockSpec((1, BLOCK, width), lambda j, asked_ref: (asked_ref[j, s], 0, 0))

    return pl.pallas_call(
        functools.partial(pack_kernel, slot),
        out_shape=jax.ShapeDtypeStruct((peers, rows, width), BF16),
        grid_spec=pltpu.PrefetchScalarGridSpec(
            num_scalar_prefetch=1,
            grid=(peers,),
            in_specs=[block_spec(s) for s in range(slot)]
            + [pl.BlockSpec((1,) + states.shape[1:], lambda j, asked_ref: (asked_ref[j, slot], 0, 0))],
            out_specs=pl.BlockSpec((1, rows, width), lambda j, asked_ref: (j, 0, 0)),
        ),
        name="pack",
    )(asked, *([block_pool] * slot), states)


def scan_kernel(x_ref, maps_ref, steps_ref, decays_ref, tokens_ref, sum_ref, local_ref, fade_ref, keep_ref):
    length = x_ref.shape[0]
    rows_i = lax.broadcasted_iota(jnp.int32, (length, length), 0)
    cols_i = lax.broadcasted_iota(jnp.int32, (length, length), 1)
    causal = rows_i >= cols_i
    running = jnp.dot(
        causal.astype(F32), decays_ref[...], precision=HIGH, preferred_element_type=F32
    )
    last = running[length - 1 : length, :]
    middle = 0.5 * last
    rise = jnp.exp(running - middle)
    fall = jnp.exp(middle - running) * steps_ref[...]
    half = jnp.exp(middle)
    fade_ref[...] = jnp.exp(running)
    keep_ref[...] = jnp.exp(last)
    entry = maps_ref[:, :NSTATE]
    readout = maps_ref[:, NSTATE:]
    meeting = lax.dot_general(
        readout, entry, (((1,), (1,)), ((), ())), precision=HIGH, preferred_element_type=F32
    )
    meeting = split_rows(jnp.where(causal, meeting, 0.0))
    per = LANES // NSTATE
    tiled = jnp.concatenate([entry] * per, 1)
    tiled_high = tiled.astype(BF16)
    tiled_low = (tiled - tiled_high.astype(F32)).astype(BF16)
    tiled = jnp.concatenate([tiled_high, tiled_low], 1)
    sub = lax.broadcasted_iota(jnp.int32, (LANES, LANES), 0)
    lane = lax.broadcasted_iota(jnp.int32, (LANES, LANES), 1)
    own = (sub % per) == (lane // NSTATE)
    heads_per = LANES // SSM_DIM
    state_rows = LANES // per
    for q in range(x_ref.shape[1] // LANES):
        cols = slice(q * LANES, (q + 1) * LANES)
        pair = slice(q * heads_per, (q + 1) * heads_per)
        drive = (x_ref[:, cols].astype(F32) * spread(fall[:, pair], SSM_DIM)).astype(BF16)
        both = jnp.dot(meeting, drive, preferred_element_type=F32)
        part = both[:length] + both[length:]
        sum_ref[:, cols] = tokens_ref[:, cols].astype(F32) + part * spread(rise[:, pair], SSM_DIM)
        outer = lax.dot_general(
            drive, tiled, (((0,), (0,)), ((), ())), preferred_element_type=F32
        )
        outer = jnp.where(own, outer[:, :LANES] + outer[:, LANES:], 0.0)
        folded = jnp.sum(outer.reshape(state_rows, per, LANES), axis=1)
        upper = lax.broadcasted_iota(jnp.int32, (state_rows, LANES), 0) < state_rows // 2
        scale = jnp.where(
            upper,
            jnp.broadcast_to(half[:, q * heads_per : q * heads_per + 1], (state_rows, LANES)),
            jnp.broadcast_to(half[:, q * heads_per + 1 : q * heads_per + 2], (state_rows, LANES)),
        )
        local_ref[q * state_rows : (q + 1) * state_rows, :] = folded * scale


def scan_local(x, maps, steps, decays, tokens):
    length, width = x.shape
    return pl.pallas_call(
        scan_kernel,
        out_shape=(
            jax.ShapeDtypeStruct((length, width), F32),
            jax.ShapeDtypeStruct((width * NSTATE // LANES, LANES), F32),
            jax.ShapeDtypeStruct(steps.shape, F32),
            jax.ShapeDtypeStruct((1, steps.shape[1]), F32),
        ),
        in_specs=[VMEM] * 5,
        out_specs=(VMEM,) * 4,
        name="scan_local",
    )(x, maps, steps, decays, tokens)


def mix_kernel(
    owner_ref,
    q_ref,
    kv_ref,
    got_ref,
    known_ref,
    sum_ref,
    local_ref,
    fade_ref,
    keep_ref,
    maps_ref,
    gain_ref,
    pick_ref,
    mixed_ref,
    normed_ref,
    send_ref,
    final_ref,
    total_ref,
):
    length, width = q_ref.shape
    peers = got_ref.shape[0]
    groups = HEADS // KV_HEADS
    state_rows = width * NSTATE // kv_ref.shape[1]
    block_rows = got_ref.shape[1] - state_rows
    past = peers * block_rows
    owner = owner_ref[0]
    per = LANES // NSTATE
    fold = LANES // per
    heads_per = LANES // SSM_DIM
    readout = maps_ref[:, NSTATE:]
    readout = split_rows(jnp.concatenate([readout] * per, 1))
    sub = lax.broadcasted_iota(jnp.int32, (fold, per, LANES), 1)
    lane = lax.broadcasted_iota(jnp.int32, (fold, per, LANES), 2)
    own = sub == lane // NSTATE
    fade = fade_ref[...]
    keep = keep_ref[...]
    token = lax.broadcasted_iota(jnp.int32, (length, length), 0)
    other = lax.broadcasted_iota(jnp.int32, (length, length), 1)
    seen = jnp.concatenate(
        [
            jnp.broadcast_to(known_ref[...], (length, past)),
            jnp.where(other <= token, 0.0, -1e30).astype(F32),
        ],
        1,
    )
    seen = jnp.concatenate([seen] * groups, 0)
    half = kv_ref.shape[1] // 2
    squares = jnp.zeros((length, LANES), F32)
    for g in range(KV_HEADS):
        key_cols = slice(g * HEAD, (g + 1) * HEAD)
        value_cols = slice(half + g * HEAD, half + (g + 1) * HEAD)
        keys = jnp.concatenate(
            [got_ref[j, 0:block_rows, key_cols] for j in range(peers)] + [kv_ref[:, key_cols]], 0
        )
        values = jnp.concatenate(
            [got_ref[j, 0:block_rows, value_cols] for j in range(peers)] + [kv_ref[:, value_cols]], 0
        )
        asks = jnp.concatenate(
            [
                q_ref[:, (g * groups + i) * HEAD : (g * groups + i + 1) * HEAD]
                for i in range(groups)
            ],
            0,
        )
        scores = (
            lax.dot_general(asks, keys, (((1,), (1,)), ((), ())), preferred_element_type=F32)
            * HEAD ** (-0.5)
            + seen
        )
        top = jnp.max(scores, axis=1, keepdims=True)
        weights = jnp.exp(scores - top)
        weights = (weights * (1.0 / jnp.sum(weights, axis=1, keepdims=True))).astype(BF16)
        attended = jnp.dot(weights, values, preferred_element_type=F32)
        for i in range(groups):
            q = g * groups + i
            cols = slice(q * LANES, (q + 1) * LANES)
            per_side = state_rows // fold
            rows_at = block_rows + (q % per_side) * fold
            start = got_ref[
                owner, rows_at : rows_at + fold, (q // per_side) * LANES : (q // per_side + 1) * LANES
            ].astype(F32)
            wide = jnp.where(own, jnp.broadcast_to(start[:, None, :], (fold, per, LANES)), 0.0)
            wide = wide.reshape(LANES, LANES).astype(BF16)
            both = lax.dot_general(
                readout, wide, (((1,), (1,)), ((), ())), preferred_element_type=F32
            )
            pair = slice(q * heads_per, (q + 1) * heads_per)
            carried = (both[:length] + both[length:]) * spread(fade[:, pair], SSM_DIM)
            upper = lax.broadcasted_iota(jnp.int32, (fold, LANES), 0) < fold // 2
            scale = jnp.where(
                upper,
                jnp.broadcast_to(keep[:, q * heads_per : q * heads_per + 1], (fold, LANES)),
                jnp.broadcast_to(keep[:, q * heads_per + 1 : q * heads_per + 2], (fold, LANES)),
            )
            final_ref[q * fold : (q + 1) * fold, :] = (
                scale * start + local_ref[q * fold : (q + 1) * fold, :]
            )
            mixed = (sum_ref[:, cols] + attended[i * length : (i + 1) * length] + carried).astype(BF16)
            mixed_ref[:, cols] = mixed
            mixed = mixed.astype(F32)
            total_ref[:, cols] = mixed
            squares = squares + mixed * mixed
    mean = jnp.sum(squares, axis=1, keepdims=True) * (1.0 / width)
    scale = lax.rsqrt(mean + 1e-05)
    step = 4 * LANES
    for q in range(width // step):
        cols = slice(q * step, (q + 1) * step)
        normed = (total_ref[:, cols] * scale * gain_ref[:, cols]).astype(BF16)
        normed_ref[:, cols] = normed
        send_ref[:, cols] = jnp.dot(
            pick_ref[...], normed, preferred_element_type=F32
        ).astype(BF16)


def mix(owner, queries, keys_values, got, known, sums, local, fade, keep, maps, gain, pick):
    length, width = queries.shape
    return pl.pallas_call(
        mix_kernel,
        out_shape=(
            jax.ShapeDtypeStruct((length, width), BF16),
            jax.ShapeDtypeStruct((length, width), BF16),
            jax.ShapeDtypeStruct((pick.shape[0], width), BF16),
            jax.ShapeDtypeStruct(local.shape, F32),
        ),
        in_specs=[SMEM] + [VMEM] * 11,
        out_specs=(VMEM,) * 4,
        scratch_shapes=[pltpu.VMEM((length, width), F32)],
        name="mix",
    )(owner, queries, keys_values, got, known, sums, local, fade, keep, maps, gain, pick)


def stream_kernel(body, arrays, chunks, *refs):
    consts = len(refs) - 2 * arrays - 4
    sources = refs[:arrays]
    fixed = refs[arrays : arrays + consts]
    out_ref = refs[arrays + consts]
    held = refs[arrays + consts + 1 : 2 * arrays + consts + 1]
    made, in_sems, out_sems = refs[2 * arrays + consts + 1 :]
    step = out_ref.shape[1] // chunks

    def inward(k, c):
        cols = pl.ds(c * step, step)
        return pltpu.make_async_copy(
            sources[k].at[:, cols], held[k].at[:, cols], in_sems.at[k, c]
        )

    def outward(c):
        cols = pl.ds(c * step, step)
        return pltpu.make_async_copy(made.at[:, cols], out_ref.at[:, cols], out_sems.at[c])

    for c in range(chunks):
        for k in range(arrays):
            inward(k, c).start()
    constants = [ref[...] for ref in fixed]
    for c in range(chunks):
        cols = slice(c * step, (c + 1) * step)
        for k in range(arrays):
            inward(k, c).wait()
        made[:, cols] = body([ref[:, cols] for ref in held], *constants)
        outward(c).start()
    for c in range(chunks):
        outward(c).wait()


def stream(body, arrays, consts, rows, chunks=4):
    width = arrays[0].shape[1]
    anywhere = pl.BlockSpec(memory_space=pl.ANY)
    moved = sum(array.shape[0] for array in arrays) + rows
    return pl.pallas_call(
        functools.partial(stream_kernel, body, len(arrays), chunks),
        out_shape=jax.ShapeDtypeStruct((rows, width), BF16),
        in_specs=[anywhere] * len(arrays) + [VMEM] * len(consts),
        out_specs=anywhere,
        scratch_shapes=[pltpu.VMEM(array.shape, array.dtype) for array in arrays]
        + [
            pltpu.VMEM((rows, width), BF16),
            pltpu.SemaphoreType.DMA((len(arrays), chunks)),
            pltpu.SemaphoreType.DMA((chunks,)),
        ],
        cost_estimate=pl.CostEstimate(
            flops=2 * moved * width, bytes_accessed=2 * moved * width, transcendentals=0
        ),
    )(*arrays, *consts)


def choose(rows, pick):
    def body(parts, pick):
        return jnp.dot(pick, parts[0], preferred_element_type=F32).astype(BF16)

    return stream(body, [rows], [pick], pick.shape[0])


def weighed(parts, weights):
    both = jnp.dot(weights, parts, preferred_element_type=F32)
    length = weights.shape[0] // 2
    return both[:length] + both[length:]


def combine(parts, weights):
    def body(held, weights):
        return weighed(held[0], weights).astype(BF16)

    return stream(body, [parts], [weights], weights.shape[0] // 2)


def finish(parts, weights, mixed, sums):
    def body(held, weights):
        total = weighed(held[0], weights)
        for far in held[2:]:
            total = total + far.astype(F32)
        return (held[1].astype(F32) + total).astype(BF16)

    return stream(body, [parts, mixed] + sums, [weights], mixed.shape[0])


def join(first, others):
    if not others:
        return first

    def body(held):
        return sum(part.astype(F32) for part in held).astype(BF16)

    return stream(body, [first] + others, [], first.shape[0])


def targets(expert_list, experts):
    capacity = expert_list.shape[0] // experts
    onehot = (expert_list[:, None] == jnp.arange(experts, dtype=jnp.int32)[None, :]).astype(F32)
    number = expert_list.shape[0]
    places = jnp.arange(number, dtype=jnp.int32)
    earlier = (places[:, None] > places[None, :]).astype(F32)
    before = jnp.dot(earlier, onehot, preferred_element_type=F32)
    slot = jnp.sum(before * onehot, axis=1).astype(jnp.int32)
    return expert_list * capacity + slot


def one_hots(expert_list, experts):
    target = targets(expert_list, experts).reshape(-1, 2)
    places = jnp.arange(expert_list.shape[0], dtype=jnp.int32)
    return target[:, :, None] == places[None, None, :]


def picker(hot):
    return jnp.any(hot, axis=1).T.astype(BF16)


def gate_weights(rows, router_weight, expert_ids, hot):
    logits = jnp.dot(rows, router_weight, preferred_element_type=F32)
    named = expert_ids[:, :, None] == jnp.arange(router_weight.shape[1], dtype=jnp.int32)
    chosen = jnp.sum(jnp.where(named, logits[:, None, :], 0.0), axis=2)
    lifted = jax.nn.sigmoid(chosen)
    gates = lifted / jnp.sum(lifted, axis=1, keepdims=True)
    weights = jnp.sum(jnp.where(hot, gates[:, :, None], 0.0), axis=1)
    return split_rows(weights)


def expert_kernel(count, first, *refs):
    sources = refs[:count]
    up_ref, down_ref = refs[count : count + 2]
    outs = refs[count + 2 : 2 * count + 2]
    rows_ref, hidden_ref = refs[2 * count + 2 :]
    step = pl.program_id(0)
    tile = up_ref.shape[1]
    each = sources[0].shape[0]

    @pl.when(step == 0)
    def _():
        for k in range(count):
            rows_ref[k * each : (k + 1) * each, :] = sources[k][...]

    @pl.when(step < first)
    def _():
        lifted = jnp.dot(rows_ref[...], up_ref[...], preferred_element_type=F32)
        cols = pl.ds(pl.multiple_of(jnp.minimum(step, first - 1) * tile, tile), tile)
        hidden_ref[:, cols] = (lifted / (1.0 + jnp.exp(-lifted))).astype(BF16)

    @pl.when(step >= first)
    def _():
        part = jnp.dot(hidden_ref[...], down_ref[...], preferred_element_type=F32).astype(BF16)
        for k in range(count):
            outs[k][...] = part[k * each : (k + 1) * each]


def apply_expert(chunks, up_local, down_local):
    count = len(chunks)
    each, width = chunks[0].shape
    hidden = up_local.shape[1]
    tile = next(t for t in (896, 512, 256, 128) if hidden % t == 0)
    wide = 8 * LANES
    first = hidden // tile
    return pl.pallas_call(
        functools.partial(expert_kernel, count, first),
        out_shape=[jax.ShapeDtypeStruct((each, width), BF16)] * count,
        grid=(first + width // wide,),
        in_specs=[pl.BlockSpec((each, width), lambda i: (0, 0))] * count
        + [
            pl.BlockSpec((width, tile), lambda i: (0, jnp.minimum(i, first - 1))),
            pl.BlockSpec((hidden, wide), lambda i: (0, jnp.maximum(i - first, 0))),
        ],
        out_specs=[pl.BlockSpec((each, wide), lambda i: (0, jnp.maximum(i - first, 0)))] * count,
        scratch_shapes=[
            pltpu.VMEM((count * each, width), BF16),
            pltpu.VMEM((count * each, hidden), BF16),
        ],
        cost_estimate=pl.CostEstimate(
            flops=4 * count * each * width * hidden,
            bytes_accessed=4 * width * hidden + 4 * count * each * width,
            transcendentals=count * each * hidden,
        ),
        name="expert",
    )(*chunks, up_local, down_local)


def local(
    tokens,
    queries,
    keys_values,
    scan_input,
    state_maps,
    step_size,
    step_decay,
    block_pool,
    state_pool,
    block_holder,
    block_index,
    cached_blocks,
    state_holder,
    state_index,
    norm_gain,
    router_weight,
    expert_ids,
    up_weight,
    down_weight,
):
    peers = lax.axis_size("dp")
    columns = lax.axis_size("expert")
    near = peers // 2

    def route(turn, side):
        return [
            (h * near + i, (h + side) % 2 * near + (i + turn) % near)
            for h in range(2)
            for i in range(near)
        ]

    experts = router_weight.shape[1]
    holders = block_holder[0]
    indices = block_index[0]
    entries = holders.shape[0]
    slot = entries // peers

    def move(rows, turn, side):
        return lax.ppermute(rows, "dp", route(turn, side))

    def swap_rows(rows):
        blocks = rows.reshape(columns, -1, rows.shape[-1])
        moved = lax.all_to_all(blocks, "expert", split_axis=0, concat_axis=0, tiled=True)
        return moved.reshape(rows.shape)

    places = jnp.arange(entries, dtype=jnp.int32)
    same = holders[:, None] == holders[None, :]
    rank = jnp.sum((same & (places[None, :] < places[:, None])).astype(jnp.int32), axis=1)
    seat = holders * slot + rank
    at_seat = seat[None, :] == places[:, None]
    wanted = jnp.sum(jnp.where(at_seat, indices[None, :], 0), axis=1)
    entry = jnp.sum(jnp.where(at_seat, places[None, :], 0), axis=1)
    known = jnp.where(entry < cached_blocks[0], 0.0, -1e30).astype(F32)
    known = jnp.repeat(known, BLOCK)[None, :]
    state_wanted = jnp.broadcast_to(state_index[0], (peers, 1))
    mine = expert_ids.reshape(-1)
    ask = jnp.concatenate(
        [
            wanted.reshape(peers, slot),
            state_wanted,
            jnp.broadcast_to(mine[None], (peers, mine.shape[0])),
        ],
        1,
    )
    asked = lax.all_to_all(ask, "dp", split_axis=0, concat_axis=0, tiled=True)
    place = lax.axis_index("dp")

    def names_of(turn):
        source = (place // near + 1) % 2 * near + (place % near + near - turn) % near
        return lax.dynamic_index_in_dim(asked[:, slot + 1 :], source, 0, keepdims=False)

    states = state_pool.reshape(state_pool.shape[0], -1, LANES).astype(BF16)
    packed = pack(asked[:, : slot + 1], block_pool, states)
    got = lax.all_to_all(packed, "dp", split_axis=0, concat_axis=0, tiled=True)

    hot = one_hots(mine, experts)
    pick = picker(hot)
    sums, from_inputs, fade, keep = scan_local(
        scan_input, state_maps, step_size, step_decay, tokens
    )
    mixed, normed, send, final_state = mix(
        state_holder,
        queries,
        keys_values,
        got,
        known,
        sums,
        from_inputs,
        fade,
        keep,
        state_maps,
        norm_gain[None, :],
        pick,
    )
    up_local = up_weight[0]
    down_local = down_weight[0]

    def gates(rows, names, hots):
        return gate_weights(rows, router_weight, names.reshape(expert_ids.shape), hots)

    far_rows = [move(normed, 0, 1)]
    near_in = swap_rows(send)
    near_moved = [move(near_in, turn, 0) for turn in range(1, near)]
    far_rows += [move(far_rows[0], turn, 0) for turn in range(1, near)]
    far_names = [names_of(turn) for turn in range(near)]
    far_hots = [one_hots(names, experts) for names in far_names]
    far_in = []
    for turn in range(near):
        chosen = choose(far_rows[turn], picker(far_hots[turn]))
        far_in.append(swap_rows(chosen))

    near_out, first_out = apply_expert([near_in, far_in[0]], up_local, down_local)
    moved_out, far_out = [], [first_out]
    if near > 1:
        moved_out += apply_expert(near_moved, up_local, down_local)
        far_out += apply_expert(far_in[1:], up_local, down_local)

    far_sums = []
    for turn in range(near):
        weights = gates(far_rows[turn], far_names[turn], far_hots[turn])
        back = swap_rows(far_out[turn])
        part = combine(back, weights)
        far_sums.append(move(part, near - turn, 1))
    moved_back = [move(rows, near - turn, 0) for turn, rows in enumerate(moved_out, 1)]
    joined = join(near_out, moved_back)
    near_back = swap_rows(joined)
    layer_out = finish(near_back, gates(normed, mine, hot), mixed, far_sums)
    return (layer_out, final_state.reshape(1, -1))


def solution(mesh):
    placed = (
        P(("dp", "expert"), None),
        P(("dp", "expert"), None),
        P(("dp", "expert"), None),
        P(("dp", "expert"), None),
        P(("dp", "expert"), None),
        P(("dp", "expert"), None),
        P(("dp", "expert"), None),
        P(("dp", "expert"), None, None),
        P(("dp", "expert"), None),
        P(("dp", "expert"), None),
        P(("dp", "expert"), None),
        P(("dp", "expert")),
        P(("dp", "expert")),
        P(("dp", "expert")),
        P(),
        P(),
        P(("dp", "expert"), None),
        P("expert", None, "dp"),
        P("expert", "dp", None),
    )
    return jax.shard_map(
        local,
        mesh=mesh,
        in_specs=placed,
        out_specs=(P(("dp", "expert"), None), P(("dp", "expert"), None)),
        check_vma=False,
    )
```

```python
import functools

import jax
import jax.numpy as jnp
from jax import lax
from jax.experimental import pallas as pl
from jax.experimental.pallas import tpu as pltpu
from jax.sharding import PartitionSpec as P


HEADS = 32
KV_HEADS = 8
HEAD = 128
SSM_DIM = 64
NSTATE = 16
BLOCK = 16
LANES = 128
HIGH = lax.Precision.HIGHEST
F32 = jnp.float32
BF16 = jnp.bfloat16
VMEM = pl.BlockSpec(memory_space=pltpu.VMEM)
SMEM = pl.BlockSpec(memory_space=pltpu.SMEM)


def split_rows(value):
    high = value.astype(BF16)
    low = (value - high.astype(F32)).astype(BF16)
    return jnp.concatenate([high, low], 0)


def spread(column_pair, width):
    rows = column_pair.shape[0]
    lane = lax.broadcasted_iota(jnp.int32, (rows, LANES), 1)
    return jnp.where(
        lane < width,
        jnp.broadcast_to(column_pair[:, 0:1], (rows, LANES)),
        jnp.broadcast_to(column_pair[:, 1:2], (rows, LANES)),
    )


def places_of(names):
    count = names.shape[1]
    length = count // 2
    token = lax.broadcasted_iota(jnp.int32, (length, count), 0)
    lane = lax.broadcasted_iota(jnp.int32, (length, count), 1)
    wide = jnp.broadcast_to(names.astype(F32), (length, count))
    return [
        jnp.sum(jnp.where(lane == 2 * token + j, wide, 0.0), axis=1, keepdims=True)
        for j in range(2)
    ]


def hots_of(names, capacity):
    columns = places_of(names)
    count = names.shape[1]
    length = count // 2
    lane = lax.broadcasted_iota(jnp.int32, (length, count), 1)
    expert = (lane // capacity).astype(F32)
    place = (lane % capacity).astype(F32)
    ones = [jnp.where(expert == column, 1.0, 0.0) for column in columns]
    rows = lax.broadcasted_iota(jnp.int32, (length, length), 0)
    cols = lax.broadcasted_iota(jnp.int32, (length, length), 1)
    earlier = jnp.where(rows > cols, 1.0, 0.0).astype(BF16)
    before = jnp.dot(earlier, (ones[0] + ones[1]).astype(BF16), preferred_element_type=F32)
    here = jnp.where(before == place, 1.0, 0.0)
    return [one * here for one in ones]


def weights_of(logits, hots):
    experts = logits.shape[1]
    count = hots[0].shape[1]
    sub = lax.broadcasted_iota(jnp.int32, (experts, count), 0)
    lane = lax.broadcasted_iota(jnp.int32, (experts, count), 1)
    wider = jnp.where(lane // (count // experts) == sub, 1.0, 0.0)
    wide = jnp.dot(logits, wider, precision=HIGH, preferred_element_type=F32)
    lifted = [
        lax.logistic(jnp.sum(wide * hot, axis=1, keepdims=True)) for hot in hots
    ]
    total = lifted[0] + lifted[1]
    weights = sum(hot * (lift / total) for hot, lift in zip(hots, lifted))
    return split_rows(weights)


def pack_kernel(slot, *refs):
    blocks = refs[1 : 1 + slot]
    state_ref = refs[1 + slot]
    out_ref = refs[2 + slot]
    for s in range(slot):
        out_ref[0, s * BLOCK : (s + 1) * BLOCK, :] = blocks[s][0]
    base = slot * BLOCK
    width = out_ref.shape[2]
    groups = width // LANES
    rows = state_ref.shape[1] // groups
    for b in range(groups):
        out_ref[0, base : base + rows, b * LANES : (b + 1) * LANES] = state_ref[
            0, b * rows : (b + 1) * rows, :
        ]


def pack(asked, block_pool, states):
    peers = asked.shape[0]
    slot = asked.shape[1] - 1
    width = block_pool.shape[2]
    state_rows = states.shape[1] * LANES // width
    rows = slot * BLOCK + state_rows

    def block_spec(s):
        return pl.BlockSpec((1, BLOCK, width), lambda j, asked_ref: (asked_ref[j, s], 0, 0))

    return pl.pallas_call(
        functools.partial(pack_kernel, slot),
        out_shape=jax.ShapeDtypeStruct((peers, rows, width), BF16),
        grid_spec=pltpu.PrefetchScalarGridSpec(
            num_scalar_prefetch=1,
            grid=(peers,),
            in_specs=[block_spec(s) for s in range(slot)]
            + [pl.BlockSpec((1,) + states.shape[1:], lambda j, asked_ref: (asked_ref[j, slot], 0, 0))],
            out_specs=pl.BlockSpec((1, rows, width), lambda j, asked_ref: (j, 0, 0)),
        ),
        compiler_params=pltpu.CompilerParams(vmem_limit_bytes=8 << 20),
        name="pack",
    )(asked, *([block_pool] * slot), states)


def scan_kernel(x_ref, maps_ref, steps_ref, decays_ref, tokens_ref, sum_ref, local_ref, fade_ref, keep_ref):
    length = x_ref.shape[0]
    rows_i = lax.broadcasted_iota(jnp.int32, (length, length), 0)
    cols_i = lax.broadcasted_iota(jnp.int32, (length, length), 1)
    causal = rows_i >= cols_i
    running = jnp.dot(
        causal.astype(F32), decays_ref[...], precision=HIGH, preferred_element_type=F32
    )
    last = running[length - 1 : length, :]
    middle = 0.5 * last
    rise = jnp.exp(running - middle)
    fall = jnp.exp(middle - running) * steps_ref[...]
    half = jnp.exp(middle)
    fade_ref[...] = jnp.exp(running)
    keep_ref[...] = jnp.exp(last)
    entry = maps_ref[:, :NSTATE]
    readout = maps_ref[:, NSTATE:]
    meeting = lax.dot_general(
        readout, entry, (((1,), (1,)), ((), ())), precision=HIGH, preferred_element_type=F32
    )
    meeting = split_rows(jnp.where(causal, meeting, 0.0))
    per = LANES // NSTATE
    tiled = jnp.concatenate([entry] * per, 1)
    tiled_high = tiled.astype(BF16)
    tiled_low = (tiled - tiled_high.astype(F32)).astype(BF16)
    tiled = jnp.concatenate([tiled_high, tiled_low], 1)
    sub = lax.broadcasted_iota(jnp.int32, (LANES, LANES), 0)
    lane = lax.broadcasted_iota(jnp.int32, (LANES, LANES), 1)
    own = (sub % per) == (lane // NSTATE)
    heads_per = LANES // SSM_DIM
    state_rows = LANES // per
    for q in range(x_ref.shape[1] // LANES):
        cols = slice(q * LANES, (q + 1) * LANES)
        pair = slice(q * heads_per, (q + 1) * heads_per)
        drive = (x_ref[:, cols].astype(F32) * spread(fall[:, pair], SSM_DIM)).astype(BF16)
        both = jnp.dot(meeting, drive, preferred_element_type=F32)
        part = both[:length] + both[length:]
        sum_ref[:, cols] = tokens_ref[:, cols].astype(F32) + part * spread(rise[:, pair], SSM_DIM)
        outer = lax.dot_general(
            drive, tiled, (((0,), (0,)), ((), ())), preferred_element_type=F32
        )
        outer = jnp.where(own, outer[:, :LANES] + outer[:, LANES:], 0.0)
        folded = jnp.sum(outer.reshape(state_rows, per, LANES), axis=1)
        upper = lax.broadcasted_iota(jnp.int32, (state_rows, LANES), 0) < state_rows // 2
        scale = jnp.where(
            upper,
            jnp.broadcast_to(half[:, q * heads_per : q * heads_per + 1], (state_rows, LANES)),
            jnp.broadcast_to(half[:, q * heads_per + 1 : q * heads_per + 2], (state_rows, LANES)),
        )
        local_ref[q * state_rows : (q + 1) * state_rows, :] = folded * scale


def scan_local(x, maps, steps, decays, tokens):
    length, width = x.shape
    return pl.pallas_call(
        scan_kernel,
        out_shape=(
            jax.ShapeDtypeStruct((length, width), F32),
            jax.ShapeDtypeStruct((width * NSTATE // LANES, LANES), F32),
            jax.ShapeDtypeStruct(steps.shape, F32),
            jax.ShapeDtypeStruct((1, steps.shape[1]), F32),
        ),
        in_specs=[VMEM] * 5,
        out_specs=(VMEM,) * 4,
        compiler_params=pltpu.CompilerParams(vmem_limit_bytes=56 << 20),
        name="scan_local",
    )(x, maps, steps, decays, tokens)


def mix_kernel(
    owner_ref,
    q_ref,
    kv_ref,
    got_ref,
    known_ref,
    sum_ref,
    local_ref,
    fade_ref,
    keep_ref,
    maps_ref,
    gain_ref,
    names_ref,
    router_ref,
    mixed_out,
    normed_ref,
    send_out,
    final_ref,
    weights_ref,
    total_ref,
    mixed_ref,
    send_ref,
    mixed_sem,
    send_sems,
):
    length, width = q_ref.shape
    peers = got_ref.shape[0]
    groups = HEADS // KV_HEADS
    state_rows = width * NSTATE // kv_ref.shape[1]
    block_rows = got_ref.shape[1] - state_rows
    past = peers * block_rows
    owner = owner_ref[0]
    per = LANES // NSTATE
    fold = LANES // per
    heads_per = LANES // SSM_DIM
    readout = maps_ref[:, NSTATE:]
    readout = split_rows(jnp.concatenate([readout] * per, 1))
    sub = lax.broadcasted_iota(jnp.int32, (fold, per, LANES), 1)
    lane = lax.broadcasted_iota(jnp.int32, (fold, per, LANES), 2)
    own = sub == lane // NSTATE
    fade = fade_ref[...]
    keep = keep_ref[...]
    token = lax.broadcasted_iota(jnp.int32, (length, length), 0)
    other = lax.broadcasted_iota(jnp.int32, (length, length), 1)
    seen = jnp.concatenate(
        [
            jnp.broadcast_to(known_ref[...], (length, past)),
            jnp.where(other <= token, 0.0, -1e30).astype(F32),
        ],
        1,
    )
    seen = jnp.concatenate([seen] * groups, 0)
    half = kv_ref.shape[1] // 2
    squares = jnp.zeros((length, LANES), F32)
    for g in range(KV_HEADS):
        key_cols = slice(g * HEAD, (g + 1) * HEAD)
        value_cols = slice(half + g * HEAD, half + (g + 1) * HEAD)
        keys = jnp.concatenate(
            [got_ref[j, 0:block_rows, key_cols] for j in range(peers)] + [kv_ref[:, key_cols]], 0
        )
        values = jnp.concatenate(
            [got_ref[j, 0:block_rows, value_cols] for j in range(peers)] + [kv_ref[:, value_cols]], 0
        )
        asks = jnp.concatenate(
            [
                q_ref[:, (g * groups + i) * HEAD : (g * groups + i + 1) * HEAD]
                for i in range(groups)
            ],
            0,
        )
        scores = (
            lax.dot_general(asks, keys, (((1,), (1,)), ((), ())), preferred_element_type=F32)
            * HEAD ** (-0.5)
            + seen
        )
        top = jnp.max(scores, axis=1, keepdims=True)
        weights = jnp.exp(scores - top)
        weights = (weights * (1.0 / jnp.sum(weights, axis=1, keepdims=True))).astype(BF16)
        attended = jnp.dot(weights, values, preferred_element_type=F32)
        for i in range(groups):
            q = g * groups + i
            cols = slice(q * LANES, (q + 1) * LANES)
            per_side = state_rows // fold
            rows_at = block_rows + (q % per_side) * fold
            start = got_ref[
                owner, rows_at : rows_at + fold, (q // per_side) * LANES : (q // per_side + 1) * LANES
            ].astype(F32)
            wide = jnp.where(own, jnp.broadcast_to(start[:, None, :], (fold, per, LANES)), 0.0)
            wide = wide.reshape(LANES, LANES).astype(BF16)
            both = lax.dot_general(
                readout, wide, (((1,), (1,)), ((), ())), preferred_element_type=F32
            )
            pair = slice(q * heads_per, (q + 1) * heads_per)
            carried = (both[:length] + both[length:]) * spread(fade[:, pair], SSM_DIM)
            upper = lax.broadcasted_iota(jnp.int32, (fold, LANES), 0) < fold // 2
            scale = jnp.where(
                upper,
                jnp.broadcast_to(keep[:, q * heads_per : q * heads_per + 1], (fold, LANES)),
                jnp.broadcast_to(keep[:, q * heads_per + 1 : q * heads_per + 2], (fold, LANES)),
            )
            final_ref[q * fold : (q + 1) * fold, :] = (
                scale * start + local_ref[q * fold : (q + 1) * fold, :]
            )
            mixed = (sum_ref[:, cols] + attended[i * length : (i + 1) * length] + carried).astype(BF16)
            mixed_ref[:, cols] = mixed
            mixed = mixed.astype(F32)
            total_ref[:, cols] = mixed
            squares = squares + mixed * mixed
    mixed_copy = pltpu.make_async_copy(mixed_ref, mixed_out, mixed_sem)
    mixed_copy.start()
    send_copies = []
    mean = jnp.sum(squares, axis=1, keepdims=True) * (1.0 / width)
    scale = lax.rsqrt(mean + 1e-05)
    experts = router_ref.shape[0]
    hots = hots_of(names_ref[...], names_ref.shape[1] // experts)
    pick = (hots[0] + hots[1]).astype(BF16)
    logits = jnp.zeros((length, experts), F32)
    step = 4 * LANES
    for q in range(width // step):
        cols = slice(q * step, (q + 1) * step)
        normed = (total_ref[:, cols] * scale * gain_ref[:, cols]).astype(BF16)
        normed_ref[:, cols] = normed
        send_ref[:, cols] = lax.dot_general(
            pick, normed, (((0,), (0,)), ((), ())), preferred_element_type=F32
        ).astype(BF16)
        send_copies.append(
            pltpu.make_async_copy(send_ref.at[:, cols], send_out.at[:, cols], send_sems.at[q])
        )
        send_copies[-1].start()
        logits = logits + lax.dot_general(
            normed, router_ref[:, cols], (((1,), (1,)), ((), ())), preferred_element_type=F32
        )
    weights_ref[...] = weights_of(logits, hots)
    mixed_copy.wait()
    for copy in send_copies:
        copy.wait()


def mix(owner, *arrays):
    queries, local, names = arrays[0], arrays[5], arrays[10]
    length, width = queries.shape
    count = names.shape[1]
    anywhere = pl.BlockSpec(memory_space=pl.ANY)
    return pl.pallas_call(
        mix_kernel,
        out_shape=(
            pltpu.HBM((length, width), BF16),
            jax.ShapeDtypeStruct((length, width), BF16),
            pltpu.HBM((count, width), BF16),
            jax.ShapeDtypeStruct(local.shape, F32),
            jax.ShapeDtypeStruct((2 * length, count), BF16),
        ),
        in_specs=[SMEM] + [VMEM] * len(arrays),
        out_specs=(anywhere, VMEM, anywhere, VMEM, VMEM),
        scratch_shapes=[
            pltpu.VMEM((length, width), F32),
            pltpu.VMEM((length, width), BF16),
            pltpu.VMEM((count, width), BF16),
            pltpu.SemaphoreType.DMA,
            pltpu.SemaphoreType.DMA((width // (4 * LANES),)),
        ],
        compiler_params=pltpu.CompilerParams(vmem_limit_bytes=56 << 20),
        name="mix",
    )(owner, *arrays[:2], resident(arrays[2]), *arrays[3:])


def resident(array):
    return pltpu.with_memory_space_constraint(array, pltpu.VMEM)


def stream_kernel(body, arrays, chunks, *refs):
    held, fixed, out_ref = refs[:arrays], refs[arrays:-1], refs[-1]
    step = out_ref.shape[1] // chunks
    constants = [ref[...] for ref in fixed]
    for c in range(chunks):
        cols = slice(c * step, (c + 1) * step)
        out_ref[:, cols] = body([ref[:, cols] for ref in held], *constants)


def stream(body, arrays, consts, rows, chunks=4, keep=True, dtype=BF16):
    width = arrays[0].shape[1]
    moved = sum(array.shape[0] for array in arrays) + rows
    shape = (rows, width)
    return pl.pallas_call(
        functools.partial(stream_kernel, body, len(arrays), chunks),
        out_shape=pltpu.VMEM(shape, dtype) if keep else jax.ShapeDtypeStruct(shape, dtype),
        in_specs=[VMEM] * (len(arrays) + len(consts)),
        out_specs=VMEM,
        cost_estimate=pl.CostEstimate(
            flops=2 * moved * width, bytes_accessed=2 * moved * width, transcendentals=0
        ),
        compiler_params=pltpu.CompilerParams(vmem_limit_bytes=8 << 20),
    )(*[resident(array) for array in arrays], *consts)


def choose_kernel(source_ref, rows_ref, names_ref, router_ref, send_ref, weights_ref):
    experts = router_ref.shape[0]
    length, width = rows_ref.shape
    names = names_ref[pl.ds(source_ref[0], 1), :][:, : 2 * length]
    hots = hots_of(names, 2 * length // experts)
    pick = (hots[0] + hots[1]).astype(BF16)
    logits = jnp.zeros((length, experts), F32)
    step = 8 * LANES
    for q in range(width // step):
        cols = slice(q * step, (q + 1) * step)
        rows = rows_ref[:, cols]
        send_ref[:, cols] = lax.dot_general(
            pick, rows, (((0,), (0,)), ((), ())), preferred_element_type=F32
        ).astype(BF16)
        logits = logits + lax.dot_general(
            rows, router_ref[:, cols], (((1,), (1,)), ((), ())), preferred_element_type=F32
        )
    weights_ref[...] = weights_of(logits, hots)


def choose(source, rows, names, router):
    length, width = rows.shape
    return pl.pallas_call(
        choose_kernel,
        out_shape=(
            pltpu.HBM((2 * length, width), BF16),
            jax.ShapeDtypeStruct((2 * length, 2 * length), BF16),
        ),
        in_specs=[SMEM] + [VMEM] * 3,
        out_specs=(VMEM, VMEM),
        compiler_params=pltpu.CompilerParams(vmem_limit_bytes=8 << 20),
        name="choose",
    )(source, resident(rows), names, router)


def weighed(parts, weights):
    both = jnp.dot(weights, parts, preferred_element_type=F32)
    length = weights.shape[0] // 2
    return both[:length] + both[length:]


def combine(parts, weights):
    def body(held, weights):
        return weighed(held[0], weights).astype(BF16)

    return stream(body, [parts], [weights], weights.shape[0] // 2)


def settle(parts, weights, mixed):
    def body(held, weights):
        return weighed(held[0], weights)

    return stream(body, [parts], [weights], mixed.shape[0], dtype=F32)


def finish(base, mixed, sums):
    def body(held):
        total = held[0]
        for far in held[2:]:
            total = total + far.astype(F32)
        return (held[1].astype(F32) + total).astype(BF16)

    return stream(body, [base, mixed] + sums, [], mixed.shape[0], keep=False)


def join(first, others):
    if not others:
        return first

    def body(held):
        return sum(part.astype(F32) for part in held).astype(BF16)

    return stream(body, [first] + others, [], first.shape[0])


def expert_kernel(count, ahead, *refs):
    sources = refs[:count]
    up_hbm, down_hbm = refs[count : count + 2]
    outs = refs[count + 2 : 2 * count + 2]
    up_ref, down_ref, hidden_ref, made_ref, sems, out_sems = refs[2 * count + 2 :]
    each, width = sources[0].shape
    tile = 2 * LANES if up_ref.shape[1] % (2 * LANES) == 0 else LANES
    wide = 4 * LANES
    first, second = up_ref.shape[1] // tile, width // wide

    def inward(n):
        if n < first:
            cols = pl.ds(n * tile, tile)
            pair = up_hbm.at[:, cols], up_ref.at[:, cols]
        else:
            cols = pl.ds((n - first) * wide, wide)
            pair = down_hbm.at[:, cols], down_ref.at[:, cols]
        return pltpu.make_async_copy(*pair, sems.at[n])

    def outward(k, n):
        cols = pl.ds(n * wide, wide)
        return pltpu.make_async_copy(
            made_ref.at[pl.ds(k * each, each), cols], outs[k].at[:, cols], out_sems.at[k, n]
        )

    for n in range(min(ahead, first + second)):
        inward(n).start()
    if count == 1:
        rows = sources[0][...]
    else:
        rows = jnp.concatenate([source[...] for source in sources], 0)
    for n in range(first + second):
        inward(n).wait()
        if n + ahead < first + second:
            inward(n + ahead).start()
        if n < first:
            cols = slice(n * tile, (n + 1) * tile)
            lifted = jnp.dot(rows, up_ref[:, cols], preferred_element_type=F32)
            hidden_ref[:, cols] = (lifted / (1.0 + jnp.exp(-lifted))).astype(BF16)
        else:
            cols = slice((n - first) * wide, (n - first + 1) * wide)
            made_ref[:, cols] = jnp.dot(
                hidden_ref[...], down_ref[:, cols], preferred_element_type=F32
            ).astype(BF16)
            for k in range(count):
                outward(k, n - first).start()
    for n in range(second):
        for k in range(count):
            outward(k, n).wait()


def apply_expert(chunks, up_local, down_local):
    count = len(chunks)
    each, width = chunks[0].shape
    hidden = up_local.shape[1]
    anywhere = pl.BlockSpec(memory_space=pl.ANY)
    tiles = hidden // (2 * LANES if hidden % (2 * LANES) == 0 else LANES)
    outs = width // (4 * LANES)
    return pl.pallas_call(
        functools.partial(expert_kernel, count, 6),
        out_shape=[pltpu.HBM((each, width), BF16)] * count,
        in_specs=[VMEM] * count + [anywhere] * 2,
        out_specs=[anywhere] * count,
        scratch_shapes=[
            pltpu.VMEM(up_local.shape, BF16),
            pltpu.VMEM(down_local.shape, BF16),
            pltpu.VMEM((count * each, hidden), BF16),
            pltpu.VMEM((count * each, width), BF16),
            pltpu.SemaphoreType.DMA((tiles + outs,)),
            pltpu.SemaphoreType.DMA((count, outs)),
        ],
        cost_estimate=pl.CostEstimate(
            flops=4 * count * each * width * hidden,
            bytes_accessed=4 * width * hidden + 4 * count * each * width,
            transcendentals=count * each * hidden,
        ),
        compiler_params=pltpu.CompilerParams(vmem_limit_bytes=48 << 20),
        name="expert",
    )(
        *[resident(chunk) for chunk in chunks],
        pltpu.with_memory_space_constraint(up_local, pltpu.HBM),
        pltpu.with_memory_space_constraint(down_local, pltpu.HBM),
    )


def local(
    tokens,
    queries,
    keys_values,
    scan_input,
    state_maps,
    step_size,
    step_decay,
    block_pool,
    state_pool,
    block_holder,
    block_index,
    cached_blocks,
    state_holder,
    state_index,
    norm_gain,
    router_weight,
    expert_ids,
    up_weight,
    down_weight,
):
    peers = lax.axis_size("dp")
    columns = lax.axis_size("expert")
    near = peers // 2

    def route(turn, side):
        return [
            (h * near + i, (h + side) % 2 * near + (i + turn) % near)
            for h in range(2)
            for i in range(near)
        ]

    holders = block_holder[0]
    indices = block_index[0]
    entries = holders.shape[0]
    slot = entries // peers

    def move(rows, turn, side):
        return lax.ppermute(rows, "dp", route(turn, side))

    def swap_rows(rows):
        blocks = rows.reshape(columns, -1, rows.shape[-1])
        moved = lax.all_to_all(blocks, "expert", split_axis=0, concat_axis=0, tiled=True)
        return moved.reshape(rows.shape)

    places = jnp.arange(entries, dtype=jnp.int32)
    same = holders[:, None] == holders[None, :]
    rank = jnp.sum((same & (places[None, :] < places[:, None])).astype(jnp.int32), axis=1)
    seat = holders * slot + rank
    at_seat = seat[None, :] == places[:, None]
    wanted = jnp.sum(jnp.where(at_seat, indices[None, :], 0), axis=1)
    entry = jnp.sum(jnp.where(at_seat, places[None, :], 0), axis=1)
    known = jnp.where(entry < cached_blocks[0], 0.0, -1e30).astype(F32)
    known = jnp.repeat(known, BLOCK)[None, :]
    state_wanted = jnp.broadcast_to(state_index[0], (peers, 1))
    mine = expert_ids.reshape(1, -1)
    count = mine.shape[1]
    ask = jnp.concatenate(
        [
            jnp.broadcast_to(mine, (peers, count)),
            wanted.reshape(peers, slot),
            state_wanted,
        ],
        1,
    )
    asked = lax.all_to_all(ask, "dp", split_axis=0, concat_axis=0, tiled=True)
    place = lax.axis_index("dp")

    def source_of(turn):
        return (place // near + 1) % 2 * near + (place % near + near - turn) % near

    states = state_pool.reshape(state_pool.shape[0], -1, LANES).astype(BF16)
    packed = pack(asked[:, count:], block_pool, states)
    got = lax.all_to_all(packed, "dp", split_axis=0, concat_axis=0, tiled=True)

    router = router_weight.T
    sums, from_inputs, fade, keep = scan_local(
        scan_input, state_maps, step_size, step_decay, tokens
    )
    mixed, normed, send, final_state, weights = mix(
        state_holder, queries, keys_values, got, known, sums, from_inputs, fade, keep, state_maps,
        norm_gain[None, :], mine, router,
    )
    up_local, down_local = up_weight[0], down_weight[0]

    far_rows = [move(normed, 0, 1)]
    near_in = swap_rows(send)
    near_moved = [move(near_in, turn, 0) for turn in range(1, near)]
    far_rows += [move(far_rows[0], turn, 0) for turn in range(1, near)]
    far_in, far_weights = [], []
    for turn in range(near):
        chosen, gates = choose(source_of(turn)[None], far_rows[turn], asked, router)
        far_in.append(swap_rows(chosen))
        far_weights.append(gates)

    def experts_on(rows):
        return list(apply_expert(rows, up_local, down_local))

    near_out, first_out = experts_on([near_in, far_in[0]])
    moved_out, far_out = [], [first_out]
    if near > 1:
        late = experts_on(near_moved + far_in[1:])
        moved_out, far_out = late[: near - 1], far_out + late[near - 1 :]

    far_sums = []
    for turn in range(near):
        back = swap_rows(far_out[turn])
        part = combine(back, far_weights[turn])
        far_sums.append(move(part, near - turn, 1))
    moved_back = [move(rows, near - turn, 0) for turn, rows in enumerate(moved_out, 1)]
    joined = join(near_out, moved_back)
    near_back = swap_rows(joined)
    base = settle(near_back, weights, mixed)
    layer_out = finish(base, mixed, far_sums)
    return (layer_out, final_state.reshape(1, -1))


def solution(mesh):
    placed = (
        P(("dp", "expert"), None),
        P(("dp", "expert"), None),
        P(("dp", "expert"), None),
        P(("dp", "expert"), None),
        P(("dp", "expert"), None),
        P(("dp", "expert"), None),
        P(("dp", "expert"), None),
        P(("dp", "expert"), None, None),
        P(("dp", "expert"), None),
        P(("dp", "expert"), None),
        P(("dp", "expert"), None),
        P(("dp", "expert")),
        P(("dp", "expert")),
        P(("dp", "expert")),
        P(),
        P(),
        P(("dp", "expert"), None),
        P("expert", None, "dp"),
        P("expert", "dp", None),
    )
    return jax.shard_map(
        local,
        mesh=mesh,
        in_specs=placed,
        out_specs=(P(("dp", "expert"), None), P(("dp", "expert"), None)),
        check_vma=False,
    )
```

```python
import functools

import jax
import jax.numpy as jnp
from jax import lax
from jax.experimental import pallas as pl
from jax.experimental.pallas import tpu as pltpu
from jax.sharding import PartitionSpec as P


HEADS = 32
KV_HEADS = 8
HEAD = 128
SSM_DIM = 64
NSTATE = 16
BLOCK = 16
LANES = 128
UP_SHARES = (1, 2, 2, 2)
DOWN_SHARES = (4, 2, 1, 1)
HIGH = lax.Precision.HIGHEST
F32 = jnp.float32
BF16 = jnp.bfloat16
VMEM = pl.BlockSpec(memory_space=pltpu.VMEM)
SMEM = pl.BlockSpec(memory_space=pltpu.SMEM)


def split_rows(value):
    high = value.astype(BF16)
    low = (value - high.astype(F32)).astype(BF16)
    return jnp.concatenate([high, low], 0)


def spread(column_pair, width):
    rows = column_pair.shape[0]
    lane = lax.broadcasted_iota(jnp.int32, (rows, LANES), 1)
    return jnp.where(
        lane < width,
        jnp.broadcast_to(column_pair[:, 0:1], (rows, LANES)),
        jnp.broadcast_to(column_pair[:, 1:2], (rows, LANES)),
    )


def places_of(names):
    count = names.shape[1]
    length = count // 2
    token = lax.broadcasted_iota(jnp.int32, (length, count), 0)
    lane = lax.broadcasted_iota(jnp.int32, (length, count), 1)
    wide = jnp.broadcast_to(names.astype(F32), (length, count))
    return [
        jnp.sum(jnp.where(lane == 2 * token + j, wide, 0.0), axis=1, keepdims=True)
        for j in range(2)
    ]


def hots_of(names, capacity):
    columns = places_of(names)
    count = names.shape[1]
    length = count // 2
    lane = lax.broadcasted_iota(jnp.int32, (length, count), 1)
    expert = (lane // capacity).astype(F32)
    place = (lane % capacity).astype(F32)
    ones = [jnp.where(expert == column, 1.0, 0.0) for column in columns]
    rows = lax.broadcasted_iota(jnp.int32, (length, length), 0)
    cols = lax.broadcasted_iota(jnp.int32, (length, length), 1)
    earlier = jnp.where(rows > cols, 1.0, 0.0).astype(BF16)
    before = jnp.dot(earlier, (ones[0] + ones[1]).astype(BF16), preferred_element_type=F32)
    here = jnp.where(before == place, 1.0, 0.0)
    return [one * here for one in ones]


def weights_of(logits, hots):
    experts = logits.shape[1]
    count = hots[0].shape[1]
    sub = lax.broadcasted_iota(jnp.int32, (experts, count), 0)
    lane = lax.broadcasted_iota(jnp.int32, (experts, count), 1)
    wider = jnp.where(lane // (count // experts) == sub, 1.0, 0.0)
    wide = jnp.dot(logits, wider, precision=HIGH, preferred_element_type=F32)
    lifted = [
        lax.logistic(jnp.sum(wide * hot, axis=1, keepdims=True)) for hot in hots
    ]
    total = lifted[0] + lifted[1]
    weights = sum(hot * (lift / total) for hot, lift in zip(hots, lifted))
    return split_rows(weights)


def turned(row):
    count = row.shape[1]
    sub = lax.broadcasted_iota(jnp.int32, (count, count), 0)
    lane = lax.broadcasted_iota(jnp.int32, (count, count), 1)
    return jnp.sum(
        jnp.where(sub == lane, jnp.broadcast_to(row, (count, count)), 0.0), axis=1, keepdims=True
    )


def plan_kernel(slot, holders_ref, indices_ref, cached_ref, state_ref, names_ref, ask_ref, known_ref):
    peers = ask_ref.shape[0]
    entries = holders_ref.shape[1]
    holders = holders_ref[...].astype(F32)
    square = (entries, entries)
    sub = lax.broadcasted_iota(jnp.int32, square, 0)
    lane = lax.broadcasted_iota(jnp.int32, square, 1)
    same = jnp.where(
        (turned(holders) == jnp.broadcast_to(holders, square)) & (sub < lane), 1.0, 0.0
    )
    seats = turned(holders * slot + jnp.sum(same, axis=0, keepdims=True))
    indices = turned(indices_ref[...].astype(F32))
    length = names_ref.shape[1]
    count = 2 * length
    names = [turned(names_ref[j : j + 1, :].astype(F32)) for j in range(2)]
    token = lax.broadcasted_iota(jnp.int32, (length, count), 0)
    at = lax.broadcasted_iota(jnp.int32, (length, count), 1)
    laid = sum(
        jnp.where(at == 2 * token + j, jnp.broadcast_to(names[j], (length, count)), 0.0)
        for j in range(2)
    )
    laid = jnp.sum(laid, axis=0, keepdims=True)
    spots = lax.broadcasted_iota(jnp.int32, (entries, LANES), 1)
    wide = jnp.broadcast_to(indices, (entries, LANES))
    for j in range(peers):
        here = (seats == (spots + j * slot).astype(F32)) & (spots < slot)
        asks = jnp.sum(jnp.where(here, wide, 0.0), axis=0, keepdims=True)
        asks = jnp.where(spots[:1] == slot, state_ref[0].astype(F32), asks)
        ask_ref[j, 0:1, :] = jnp.concatenate([laid, asks], 1).astype(jnp.int32)
    past = known_ref.shape[1]
    spots = lax.broadcasted_iota(jnp.int32, (entries, past), 1) // BLOCK
    order = lax.broadcasted_iota(jnp.int32, (entries, past), 0).astype(F32)
    entry = jnp.sum(
        jnp.where(seats == spots.astype(F32), order, 0.0), axis=0, keepdims=True
    )
    known_ref[...] = jnp.where(entry < cached_ref[0].astype(F32), 0.0, -1e30)


def plan(peers, holders, indices, cached, state, names):
    entries = holders.shape[1]
    return pl.pallas_call(
        functools.partial(plan_kernel, entries // peers),
        out_shape=(
            jax.ShapeDtypeStruct((peers, 1, 2 * names.shape[1] + LANES), jnp.int32),
            jax.ShapeDtypeStruct((1, entries * BLOCK), F32),
        ),
        in_specs=[VMEM, VMEM, SMEM, SMEM, VMEM],
        out_specs=(VMEM, VMEM),
        name="plan",
    )(holders, indices, cached, state, names)


def pack_kernel(slot, *refs):
    blocks = refs[1 : 1 + slot]
    state_ref = refs[1 + slot]
    out_ref = refs[2 + slot]
    for s in range(slot):
        out_ref[0, s * BLOCK : (s + 1) * BLOCK, :] = blocks[s][0]
    base = slot * BLOCK
    width = out_ref.shape[2]
    groups = width // LANES
    rows = state_ref.shape[1] // groups
    for b in range(groups):
        out_ref[0, base : base + rows, b * LANES : (b + 1) * LANES] = state_ref[
            0, b * rows : (b + 1) * rows, :
        ]


def pack(asked, block_pool, states):
    peers = asked.shape[0]
    slot = asked.shape[1] - 1
    width = block_pool.shape[2]
    state_rows = states.shape[1] * LANES // width
    rows = slot * BLOCK + state_rows

    def block_spec(s):
        return pl.BlockSpec((1, BLOCK, width), lambda j, asked_ref: (asked_ref[j, s], 0, 0))

    return pl.pallas_call(
        functools.partial(pack_kernel, slot),
        out_shape=jax.ShapeDtypeStruct((peers, rows, width), BF16),
        grid_spec=pltpu.PrefetchScalarGridSpec(
            num_scalar_prefetch=1,
            grid=(peers,),
            in_specs=[block_spec(s) for s in range(slot)]
            + [pl.BlockSpec((1,) + states.shape[1:], lambda j, asked_ref: (asked_ref[j, slot], 0, 0))],
            out_specs=pl.BlockSpec((1, rows, width), lambda j, asked_ref: (j, 0, 0)),
        ),
        compiler_params=pltpu.CompilerParams(vmem_limit_bytes=8 << 20),
        name="pack",
    )(asked, *([block_pool] * slot), states)


def scan_kernel(x_ref, maps_ref, steps_ref, decays_ref, tokens_ref, sum_ref, local_ref, fade_ref, keep_ref):
    length = x_ref.shape[0]
    rows_i = lax.broadcasted_iota(jnp.int32, (length, length), 0)
    cols_i = lax.broadcasted_iota(jnp.int32, (length, length), 1)
    causal = rows_i >= cols_i
    running = jnp.dot(
        causal.astype(F32), decays_ref[...], precision=HIGH, preferred_element_type=F32
    )
    last = running[length - 1 : length, :]
    middle = 0.5 * last
    rise = jnp.exp(running - middle)
    fall = jnp.exp(middle - running) * steps_ref[...]
    half = jnp.exp(middle)
    fade_ref[...] = jnp.exp(running)
    keep_ref[...] = jnp.exp(last)
    entry = maps_ref[:, :NSTATE]
    readout = maps_ref[:, NSTATE:]
    meeting = lax.dot_general(
        readout, entry, (((1,), (1,)), ((), ())), precision=HIGH, preferred_element_type=F32
    )
    meeting = split_rows(jnp.where(causal, meeting, 0.0))
    per = LANES // NSTATE
    tiled = jnp.concatenate([entry] * per, 1)
    tiled_high = tiled.astype(BF16)
    tiled_low = (tiled - tiled_high.astype(F32)).astype(BF16)
    tiled = jnp.concatenate([tiled_high, tiled_low], 1)
    sub = lax.broadcasted_iota(jnp.int32, (LANES, LANES), 0)
    lane = lax.broadcasted_iota(jnp.int32, (LANES, LANES), 1)
    own = (sub % per) == (lane // NSTATE)
    heads_per = LANES // SSM_DIM
    state_rows = LANES // per
    for q in range(x_ref.shape[1] // LANES):
        cols = slice(q * LANES, (q + 1) * LANES)
        pair = slice(q * heads_per, (q + 1) * heads_per)
        drive = (x_ref[:, cols].astype(F32) * spread(fall[:, pair], SSM_DIM)).astype(BF16)
        both = jnp.dot(meeting, drive, preferred_element_type=F32)
        part = both[:length] + both[length:]
        sum_ref[:, cols] = tokens_ref[:, cols].astype(F32) + part * spread(rise[:, pair], SSM_DIM)
        outer = lax.dot_general(
            drive, tiled, (((0,), (0,)), ((), ())), preferred_element_type=F32
        )
        outer = jnp.where(own, outer[:, :LANES] + outer[:, LANES:], 0.0)
        folded = jnp.sum(outer.reshape(state_rows, per, LANES), axis=1)
        upper = lax.broadcasted_iota(jnp.int32, (state_rows, LANES), 0) < state_rows // 2
        scale = jnp.where(
            upper,
            jnp.broadcast_to(half[:, q * heads_per : q * heads_per + 1], (state_rows, LANES)),
            jnp.broadcast_to(half[:, q * heads_per + 1 : q * heads_per + 2], (state_rows, LANES)),
        )
        local_ref[q * state_rows : (q + 1) * state_rows, :] = folded * scale


def scan_local(x, maps, steps, decays, tokens):
    length, width = x.shape
    return pl.pallas_call(
        scan_kernel,
        out_shape=(
            jax.ShapeDtypeStruct((length, width), F32),
            jax.ShapeDtypeStruct((width * NSTATE // LANES, LANES), F32),
            jax.ShapeDtypeStruct(steps.shape, F32),
            jax.ShapeDtypeStruct((1, steps.shape[1]), F32),
        ),
        in_specs=[VMEM] * 5,
        out_specs=(VMEM,) * 4,
        compiler_params=pltpu.CompilerParams(vmem_limit_bytes=56 << 20),
        name="scan_local",
    )(x, maps, steps, decays, tokens)


def mix_kernel(
    owner_ref,
    q_ref,
    kv_ref,
    got_ref,
    known_ref,
    sum_ref,
    local_ref,
    fade_ref,
    keep_ref,
    maps_ref,
    gain_ref,
    names_ref,
    router_ref,
    mixed_out,
    normed_ref,
    send_out,
    final_ref,
    weights_ref,
    total_ref,
    mixed_ref,
    send_ref,
    mixed_sem,
    send_sems,
):
    length, width = q_ref.shape
    peers = got_ref.shape[0]
    groups = HEADS // KV_HEADS
    state_rows = width * NSTATE // kv_ref.shape[1]
    block_rows = got_ref.shape[1] - state_rows
    past = peers * block_rows
    owner = owner_ref[0]
    per = LANES // NSTATE
    fold = LANES // per
    heads_per = LANES // SSM_DIM
    readout = maps_ref[:, NSTATE:]
    readout = split_rows(jnp.concatenate([readout] * per, 1))
    sub = lax.broadcasted_iota(jnp.int32, (fold, per, LANES), 1)
    lane = lax.broadcasted_iota(jnp.int32, (fold, per, LANES), 2)
    own = sub == lane // NSTATE
    fade = fade_ref[...]
    keep = keep_ref[...]
    token = lax.broadcasted_iota(jnp.int32, (length, length), 0)
    other = lax.broadcasted_iota(jnp.int32, (length, length), 1)
    seen = jnp.concatenate(
        [
            jnp.broadcast_to(known_ref[...], (length, past)),
            jnp.where(other <= token, 0.0, -1e30).astype(F32),
        ],
        1,
    )
    seen = jnp.concatenate([seen] * groups, 0)
    half = kv_ref.shape[1] // 2
    squares = jnp.zeros((length, LANES), F32)
    for g in range(KV_HEADS):
        key_cols = slice(g * HEAD, (g + 1) * HEAD)
        value_cols = slice(half + g * HEAD, half + (g + 1) * HEAD)
        keys = jnp.concatenate(
            [got_ref[j, 0:block_rows, key_cols] for j in range(peers)] + [kv_ref[:, key_cols]], 0
        )
        values = jnp.concatenate(
            [got_ref[j, 0:block_rows, value_cols] for j in range(peers)] + [kv_ref[:, value_cols]], 0
        )
        asks = jnp.concatenate(
            [
                q_ref[:, (g * groups + i) * HEAD : (g * groups + i + 1) * HEAD]
                for i in range(groups)
            ],
            0,
        )
        scores = (
            lax.dot_general(asks, keys, (((1,), (1,)), ((), ())), preferred_element_type=F32)
            * HEAD ** (-0.5)
            + seen
        )
        top = jnp.max(scores, axis=1, keepdims=True)
        weights = jnp.exp(scores - top)
        weights = (weights * (1.0 / jnp.sum(weights, axis=1, keepdims=True))).astype(BF16)
        attended = jnp.dot(weights, values, preferred_element_type=F32)
        for i in range(groups):
            q = g * groups + i
            cols = slice(q * LANES, (q + 1) * LANES)
            per_side = state_rows // fold
            rows_at = block_rows + (q % per_side) * fold
            start = got_ref[
                owner, rows_at : rows_at + fold, (q // per_side) * LANES : (q // per_side + 1) * LANES
            ].astype(F32)
            wide = jnp.where(own, jnp.broadcast_to(start[:, None, :], (fold, per, LANES)), 0.0)
            wide = wide.reshape(LANES, LANES).astype(BF16)
            both = lax.dot_general(
                readout, wide, (((1,), (1,)), ((), ())), preferred_element_type=F32
            )
            pair = slice(q * heads_per, (q + 1) * heads_per)
            carried = (both[:length] + both[length:]) * spread(fade[:, pair], SSM_DIM)
            upper = lax.broadcasted_iota(jnp.int32, (fold, LANES), 0) < fold // 2
            scale = jnp.where(
                upper,
                jnp.broadcast_to(keep[:, q * heads_per : q * heads_per + 1], (fold, LANES)),
                jnp.broadcast_to(keep[:, q * heads_per + 1 : q * heads_per + 2], (fold, LANES)),
            )
            final_ref[q * fold : (q + 1) * fold, :] = (
                scale * start + local_ref[q * fold : (q + 1) * fold, :]
            )
            mixed = (sum_ref[:, cols] + attended[i * length : (i + 1) * length] + carried).astype(BF16)
            mixed_ref[:, cols] = mixed
            mixed = mixed.astype(F32)
            total_ref[:, cols] = mixed
            squares = squares + mixed * mixed
    mixed_copy = pltpu.make_async_copy(mixed_ref, mixed_out, mixed_sem)
    mixed_copy.start()
    send_copies = []
    mean = jnp.sum(squares, axis=1, keepdims=True) * (1.0 / width)
    scale = lax.rsqrt(mean + 1e-05)
    experts = router_ref.shape[0]
    hots = hots_of(names_ref[:, : 2 * length], 2 * length // experts)
    pick = (hots[0] + hots[1]).astype(BF16)
    logits = jnp.zeros((length, experts), F32)
    step = 4 * LANES
    for q in range(width // step):
        cols = slice(q * step, (q + 1) * step)
        normed = (total_ref[:, cols] * scale * gain_ref[:, cols]).astype(BF16)
        normed_ref[:, cols] = normed
        send_ref[:, cols] = lax.dot_general(
            pick, normed, (((0,), (0,)), ((), ())), preferred_element_type=F32
        ).astype(BF16)
        send_copies.append(
            pltpu.make_async_copy(send_ref.at[:, cols], send_out.at[:, cols], send_sems.at[q])
        )
        send_copies[-1].start()
        logits = logits + lax.dot_general(
            normed, router_ref[:, cols], (((1,), (1,)), ((), ())), preferred_element_type=F32
        )
    weights_ref[...] = weights_of(logits, hots)
    mixed_copy.wait()
    for copy in send_copies:
        copy.wait()


def mix(owner, *arrays):
    queries, local = arrays[0], arrays[5]
    length, width = queries.shape
    count = 2 * length
    anywhere = pl.BlockSpec(memory_space=pl.ANY)
    return pl.pallas_call(
        mix_kernel,
        out_shape=(
            pltpu.HBM((length, width), BF16),
            jax.ShapeDtypeStruct((length, width), BF16),
            pltpu.HBM((count, width), BF16),
            jax.ShapeDtypeStruct(local.shape, F32),
            jax.ShapeDtypeStruct((2 * length, count), BF16),
        ),
        in_specs=[SMEM] + [VMEM] * len(arrays),
        out_specs=(anywhere, VMEM, anywhere, VMEM, VMEM),
        scratch_shapes=[
            pltpu.VMEM((length, width), F32),
            pltpu.VMEM((length, width), BF16),
            pltpu.VMEM((count, width), BF16),
            pltpu.SemaphoreType.DMA,
            pltpu.SemaphoreType.DMA((width // (4 * LANES),)),
        ],
        compiler_params=pltpu.CompilerParams(vmem_limit_bytes=56 << 20),
        name="mix",
    )(owner, *arrays[:2], resident(arrays[2]), *arrays[3:])


def resident(array):
    return pltpu.with_memory_space_constraint(array, pltpu.VMEM)


def stream_kernel(body, arrays, chunks, *refs):
    held, fixed, out_ref = refs[:arrays], refs[arrays:-1], refs[-1]
    step = out_ref.shape[1] // chunks
    constants = [ref[...] for ref in fixed]
    for c in range(chunks):
        cols = slice(c * step, (c + 1) * step)
        out_ref[:, cols] = body([ref[:, cols] for ref in held], *constants)


def stream(body, arrays, consts, rows, chunks=4, keep=True, dtype=BF16):
    width = arrays[0].shape[1]
    moved = sum(array.shape[0] for array in arrays) + rows
    shape = (rows, width)
    return pl.pallas_call(
        functools.partial(stream_kernel, body, len(arrays), chunks),
        out_shape=pltpu.VMEM(shape, dtype) if keep else jax.ShapeDtypeStruct(shape, dtype),
        in_specs=[VMEM] * (len(arrays) + len(consts)),
        out_specs=VMEM,
        cost_estimate=pl.CostEstimate(
            flops=2 * moved * width, bytes_accessed=2 * moved * width, transcendentals=0
        ),
        compiler_params=pltpu.CompilerParams(vmem_limit_bytes=8 << 20),
    )(*[resident(array) for array in arrays], *consts)


def choose_kernel(source_ref, rows_ref, names_ref, router_ref, send_ref, weights_ref):
    experts = router_ref.shape[0]
    length, width = rows_ref.shape
    names = names_ref[pl.ds(source_ref[0], 1), :][:, : 2 * length]
    hots = hots_of(names, 2 * length // experts)
    pick = (hots[0] + hots[1]).astype(BF16)
    logits = jnp.zeros((length, experts), F32)
    step = 8 * LANES
    for q in range(width // step):
        cols = slice(q * step, (q + 1) * step)
        rows = rows_ref[:, cols]
        send_ref[:, cols] = lax.dot_general(
            pick, rows, (((0,), (0,)), ((), ())), preferred_element_type=F32
        ).astype(BF16)
        logits = logits + lax.dot_general(
            rows, router_ref[:, cols], (((1,), (1,)), ((), ())), preferred_element_type=F32
        )
    weights_ref[...] = weights_of(logits, hots)


def choose(source, rows, names, router):
    length, width = rows.shape
    return pl.pallas_call(
        choose_kernel,
        out_shape=(
            pltpu.HBM((2 * length, width), BF16),
            jax.ShapeDtypeStruct((2 * length, 2 * length), BF16),
        ),
        in_specs=[SMEM] + [VMEM] * 3,
        out_specs=(VMEM, VMEM),
        compiler_params=pltpu.CompilerParams(vmem_limit_bytes=8 << 20),
        name="choose",
    )(source, resident(rows), names, router)


def weighed(parts, weights):
    both = jnp.dot(weights, parts, preferred_element_type=F32)
    length = weights.shape[0] // 2
    return both[:length] + both[length:]


def combine(parts, weights):
    def body(held, weights):
        return weighed(held[0], weights).astype(BF16)

    return stream(body, [parts], [weights], weights.shape[0] // 2)


def held_kernel(body, arrays, *refs):
    held, far_ref, out_ref = refs[:arrays], refs[arrays], refs[arrays + 1]
    near_ref, made_ref, sem, out_sems = refs[arrays + 2 :]
    chunks = out_sems.shape[0]
    step = out_ref.shape[1] // chunks
    copy = pltpu.make_async_copy(far_ref, near_ref, sem)
    copy.start()
    outs = []
    for c in range(chunks):
        cols = slice(c * step, (c + 1) * step)
        made = body(cols, *held)
        if c == 0:
            copy.wait()
        made_ref[:, cols] = (made + near_ref[:, cols].astype(F32)).astype(BF16)
        outs.append(
            pltpu.make_async_copy(made_ref.at[:, cols], out_ref.at[:, cols], out_sems.at[c])
        )
        outs[-1].start()
    for out in outs:
        out.wait()


def held_call(body, arrays, far, chunks=4):
    anywhere = pl.BlockSpec(memory_space=pl.ANY)
    return pl.pallas_call(
        functools.partial(held_kernel, body, len(arrays)),
        out_shape=pltpu.HBM(far.shape, BF16),
        in_specs=[VMEM] * len(arrays) + [anywhere],
        out_specs=anywhere,
        scratch_shapes=[
            pltpu.VMEM(far.shape, BF16),
            pltpu.VMEM(far.shape, BF16),
            pltpu.SemaphoreType.DMA,
            pltpu.SemaphoreType.DMA((chunks,)),
        ],
        compiler_params=pltpu.CompilerParams(vmem_limit_bytes=16 << 20),
    )(*[resident(array) for array in arrays], pltpu.with_memory_space_constraint(far, pltpu.HBM))


def finish(parts, weights, sums, mixed):
    def body(cols, parts_ref, weights_ref, *sums_refs):
        total = weighed(parts_ref[:, cols], weights_ref[...])
        for ref in sums_refs:
            total = total + ref[:, cols].astype(F32)
        return total

    return held_call(body, [parts, weights] + sums, mixed)


def join(first, others):
    if not others:
        return first

    def body(cols, *refs):
        return sum(ref[:, cols].astype(F32) for ref in refs)

    return held_call(body, others, first)


def expert_kernel(count, ups, downs, *refs):
    sources = refs[:count]
    up_hbm, down_hbm = refs[count : count + 2]
    outs = refs[count + 2 : 2 * count + 2]
    up_ref, down_ref, hidden_ref, made_ref, sems, out_sems = refs[2 * count + 2 :]
    each, _ = sources[0].shape
    copies = [
        pltpu.make_async_copy(
            hbm.at[:, pl.ds(start, size)], ref.at[:, pl.ds(start, size)], sems.at[base + n]
        )
        for hbm, ref, blocks, base in (
            (up_hbm, up_ref, ups, 0),
            (down_hbm, down_ref, downs, len(ups)),
        )
        for n, (start, size) in enumerate(blocks)
    ]
    for copy in copies:
        copy.start()
    if count == 1:
        rows = sources[0][...]
    else:
        rows = jnp.concatenate([source[...] for source in sources], 0)
    tile = 2 * LANES
    for (start, size), copy in zip(ups, copies):
        copy.wait()
        for at in range(start, start + size, tile):
            cols = slice(at, min(at + tile, start + size))
            lifted = jnp.dot(rows, up_ref[:, cols], preferred_element_type=F32)
            hidden_ref[:, cols] = (lifted / (1.0 + jnp.exp(-lifted))).astype(BF16)
    hidden = hidden_ref[...]
    tile = 4 * LANES
    flying = []
    for n, ((start, size), copy) in enumerate(zip(downs, copies[len(ups) :])):
        copy.wait()
        for at in range(start, start + size, tile):
            cols = slice(at, at + tile)
            made_ref[:, cols] = jnp.dot(
                hidden, down_ref[:, cols], preferred_element_type=F32
            ).astype(BF16)
        for k in range(count):
            cols = pl.ds(start, size)
            flying.append(
                pltpu.make_async_copy(
                    made_ref.at[pl.ds(k * each, each), cols],
                    outs[k].at[:, cols],
                    out_sems.at[k, n],
                )
            )
            flying[-1].start()
    for copy in flying:
        copy.wait()


def blocks_of(total, shares):
    unit = total // sum(shares)
    if unit % LANES or unit * sum(shares) != total:
        return [(0, total)]
    ends = [unit * sum(shares[: n + 1]) for n in range(len(shares))]
    return [(end - unit * share, unit * share) for end, share in zip(ends, shares)]


def apply_expert(chunks, up_local, down_local):
    count = len(chunks)
    each, width = chunks[0].shape
    hidden = up_local.shape[1]
    anywhere = pl.BlockSpec(memory_space=pl.ANY)
    ups = blocks_of(hidden, UP_SHARES)
    downs = blocks_of(width, DOWN_SHARES)
    return pl.pallas_call(
        functools.partial(expert_kernel, count, ups, downs),
        out_shape=[pltpu.HBM((each, width), BF16)] * count,
        in_specs=[VMEM] * count + [anywhere] * 2,
        out_specs=[anywhere] * count,
        scratch_shapes=[
            pltpu.VMEM(up_local.shape, BF16),
            pltpu.VMEM(down_local.shape, BF16),
            pltpu.VMEM((count * each, hidden), BF16),
            pltpu.VMEM((count * each, width), BF16),
            pltpu.SemaphoreType.DMA((len(ups) + len(downs),)),
            pltpu.SemaphoreType.DMA((count, len(downs))),
        ],
        cost_estimate=pl.CostEstimate(
            flops=4 * count * each * width * hidden,
            bytes_accessed=4 * width * hidden + 4 * count * each * width,
            transcendentals=count * each * hidden,
        ),
        compiler_params=pltpu.CompilerParams(vmem_limit_bytes=50 << 20),
        name="expert",
    )(
        *[resident(chunk) for chunk in chunks],
        pltpu.with_memory_space_constraint(up_local, pltpu.HBM),
        pltpu.with_memory_space_constraint(down_local, pltpu.HBM),
    )


def local(
    tokens,
    queries,
    keys_values,
    scan_input,
    state_maps,
    step_size,
    step_decay,
    block_pool,
    state_pool,
    block_holder,
    block_index,
    cached_blocks,
    state_holder,
    state_index,
    norm_gain,
    router_weight,
    expert_ids,
    up_weight,
    down_weight,
):
    peers = lax.axis_size("dp")
    columns = lax.axis_size("expert")
    near = peers // 2

    def route(turn, side):
        return [
            (h * near + i, (h + side) % 2 * near + (i + turn) % near)
            for h in range(2)
            for i in range(near)
        ]

    def move(rows, turn, side):
        return lax.ppermute(rows, "dp", route(turn, side))

    def swap_rows(rows):
        blocks = rows.reshape(columns, -1, rows.shape[-1])
        moved = lax.all_to_all(blocks, "expert", split_axis=0, concat_axis=0, tiled=True)
        return moved.reshape(rows.shape)

    slot = block_holder.shape[1] // peers
    count = 2 * expert_ids.shape[0]
    ask, known = plan(peers, block_holder, block_index, cached_blocks, state_index, expert_ids.T)
    asked = lax.all_to_all(ask, "dp", split_axis=0, concat_axis=0, tiled=True)[:, 0]
    place = lax.axis_index("dp")

    def source_of(turn):
        return (place // near + 1) % 2 * near + (place % near + near - turn) % near

    states = state_pool.reshape(state_pool.shape[0], -1, LANES).astype(BF16)
    packed = pack(asked[:, count : count + slot + 1], block_pool, states)
    got = lax.all_to_all(packed, "dp", split_axis=0, concat_axis=0, tiled=True)

    router = router_weight.T
    sums, from_inputs, fade, keep = scan_local(
        scan_input, state_maps, step_size, step_decay, tokens
    )
    mixed, normed, send, final_state, weights = mix(
        state_holder, queries, keys_values, got, known, sums, from_inputs, fade, keep, state_maps,
        norm_gain[None, :], ask[0], router,
    )
    up_local, down_local = up_weight[0], down_weight[0]

    far_rows = [move(normed, 0, 1)]
    near_in = swap_rows(send)
    near_moved = [move(near_in, turn, 0) for turn in range(1, near)]
    far_rows += [move(far_rows[0], turn, 0) for turn in range(1, near)]
    far_in, far_weights = [], []
    for turn in range(near):
        chosen, gates = choose(source_of(turn)[None], far_rows[turn], asked, router)
        far_in.append(swap_rows(chosen))
        far_weights.append(gates)

    def experts_on(rows):
        return list(apply_expert(rows, up_local, down_local))

    near_out, first_out = experts_on([near_in, far_in[0]])
    moved_out, far_out = [], [first_out]
    if near > 1:
        late = experts_on(near_moved + far_in[1:])
        moved_out, far_out = late[: near - 1], far_out + late[near - 1 :]

    far_sums = []
    for turn in range(near):
        back = swap_rows(far_out[turn])
        part = combine(back, far_weights[turn])
        far_sums.append(move(part, near - turn, 1))
    moved_back = [move(rows, near - turn, 0) for turn, rows in enumerate(moved_out, 1)]
    joined = join(near_out, moved_back)
    near_back = swap_rows(joined)
    layer_out = finish(near_back, weights, far_sums, mixed)
    return (layer_out, final_state.reshape(1, -1))


def solution(mesh):
    placed = (
        P(("dp", "expert"), None),
        P(("dp", "expert"), None),
        P(("dp", "expert"), None),
        P(("dp", "expert"), None),
        P(("dp", "expert"), None),
        P(("dp", "expert"), None),
        P(("dp", "expert"), None),
        P(("dp", "expert"), None, None),
        P(("dp", "expert"), None),
        P(("dp", "expert"), None),
        P(("dp", "expert"), None),
        P(("dp", "expert")),
        P(("dp", "expert")),
        P(("dp", "expert")),
        P(),
        P(),
        P(("dp", "expert"), None),
        P("expert", None, "dp"),
        P("expert", "dp", None),
    )
    return jax.shard_map(
        local,
        mesh=mesh,
        in_specs=placed,
        out_specs=(P(("dp", "expert"), None), P(("dp", "expert"), None)),
        check_vma=False,
    )
```

```python
import functools
import math

import jax
import jax.numpy as jnp
from jax import lax
from jax.experimental import pallas as pl
from jax.experimental.pallas import tpu as pltpu
from jax.sharding import PartitionSpec as P


HEADS = 32
KV_HEADS = 8
HEAD = 128
SSM_DIM = 64
NSTATE = 16
BLOCK = 16
LANES = 128
UP_SHARES = (1, 2, 2, 2)
DOWN_SHARES = (4, 2, 1, 1)
HIGH = lax.Precision.HIGHEST
F32 = jnp.float32
BF16 = jnp.bfloat16
VMEM = pl.BlockSpec(memory_space=pltpu.VMEM)
SMEM = pl.BlockSpec(memory_space=pltpu.SMEM)


def split_rows(value):
    high = value.astype(BF16)
    low = (value - high.astype(F32)).astype(BF16)
    return jnp.concatenate([high, low], 0)


def spread(column_pair, width):
    rows = column_pair.shape[0]
    lane = lax.broadcasted_iota(jnp.int32, (rows, LANES), 1)
    return jnp.where(
        lane < width,
        jnp.broadcast_to(column_pair[:, 0:1], (rows, LANES)),
        jnp.broadcast_to(column_pair[:, 1:2], (rows, LANES)),
    )


def places_of(names):
    count = names.shape[1]
    length = count // 2
    token = lax.broadcasted_iota(jnp.int32, (length, count), 0)
    lane = lax.broadcasted_iota(jnp.int32, (length, count), 1)
    wide = jnp.broadcast_to(names.astype(F32), (length, count))
    return [
        jnp.sum(jnp.where(lane == 2 * token + j, wide, 0.0), axis=1, keepdims=True)
        for j in range(2)
    ]


def hots_of(names, capacity):
    columns = places_of(names)
    count = names.shape[1]
    length = count // 2
    lane = lax.broadcasted_iota(jnp.int32, (length, count), 1)
    expert = (lane // capacity).astype(F32)
    place = (lane % capacity).astype(F32)
    ones = [jnp.where(expert == column, 1.0, 0.0) for column in columns]
    rows = lax.broadcasted_iota(jnp.int32, (length, length), 0)
    cols = lax.broadcasted_iota(jnp.int32, (length, length), 1)
    earlier = jnp.where(rows > cols, 1.0, 0.0).astype(BF16)
    before = jnp.dot(earlier, (ones[0] + ones[1]).astype(BF16), preferred_element_type=F32)
    here = jnp.where(before == place, 1.0, 0.0)
    return [one * here for one in ones]


def weights_of(logits, hots):
    experts = logits.shape[1]
    count = hots[0].shape[1]
    sub = lax.broadcasted_iota(jnp.int32, (experts, count), 0)
    lane = lax.broadcasted_iota(jnp.int32, (experts, count), 1)
    wider = jnp.where(lane // (count // experts) == sub, 1.0, 0.0)
    wide = jnp.dot(logits, wider, precision=HIGH, preferred_element_type=F32)
    lifted = [
        lax.logistic(jnp.sum(wide * hot, axis=1, keepdims=True)) for hot in hots
    ]
    total = lifted[0] + lifted[1]
    weights = sum(hot * (lift / total) for hot, lift in zip(hots, lifted))
    return split_rows(weights)


def turned(row):
    count = row.shape[1]
    sub = lax.broadcasted_iota(jnp.int32, (count, count), 0)
    lane = lax.broadcasted_iota(jnp.int32, (count, count), 1)
    return jnp.sum(
        jnp.where(sub == lane, jnp.broadcast_to(row, (count, count)), 0.0), axis=1, keepdims=True
    )


def plan_kernel(slot, holders_ref, indices_ref, cached_ref, state_ref, names_ref, ask_ref, known_ref):
    peers = ask_ref.shape[0]
    entries = holders_ref.shape[1]
    holders = holders_ref[...].astype(F32)
    square = (entries, entries)
    sub = lax.broadcasted_iota(jnp.int32, square, 0)
    lane = lax.broadcasted_iota(jnp.int32, square, 1)
    same = jnp.where(
        (turned(holders) == jnp.broadcast_to(holders, square)) & (sub < lane), 1.0, 0.0
    )
    seats = turned(holders * slot + jnp.sum(same, axis=0, keepdims=True))
    indices = turned(indices_ref[...].astype(F32))
    length = names_ref.shape[1]
    count = 2 * length
    names = [turned(names_ref[j : j + 1, :].astype(F32)) for j in range(2)]
    token = lax.broadcasted_iota(jnp.int32, (length, count), 0)
    at = lax.broadcasted_iota(jnp.int32, (length, count), 1)
    laid = sum(
        jnp.where(at == 2 * token + j, jnp.broadcast_to(names[j], (length, count)), 0.0)
        for j in range(2)
    )
    laid = jnp.sum(laid, axis=0, keepdims=True)
    spots = lax.broadcasted_iota(jnp.int32, (entries, LANES), 1)
    wide = jnp.broadcast_to(indices, (entries, LANES))
    for j in range(peers):
        here = (seats == (spots + j * slot).astype(F32)) & (spots < slot)
        asks = jnp.sum(jnp.where(here, wide, 0.0), axis=0, keepdims=True)
        asks = jnp.where(spots[:1] == slot, state_ref[0].astype(F32), asks)
        ask_ref[j, 0:1, :] = jnp.concatenate([laid, asks], 1).astype(jnp.int32)
    past = known_ref.shape[1]
    spots = lax.broadcasted_iota(jnp.int32, (entries, past), 1) // BLOCK
    order = lax.broadcasted_iota(jnp.int32, (entries, past), 0).astype(F32)
    entry = jnp.sum(
        jnp.where(seats == spots.astype(F32), order, 0.0), axis=0, keepdims=True
    )
    known_ref[...] = jnp.where(entry < cached_ref[0].astype(F32), 0.0, -1e30)


def plan(peers, holders, indices, cached, state, names):
    entries = holders.shape[1]
    return pl.pallas_call(
        functools.partial(plan_kernel, entries // peers),
        out_shape=(
            jax.ShapeDtypeStruct((peers, 1, 2 * names.shape[1] + LANES), jnp.int32),
            jax.ShapeDtypeStruct((1, entries * BLOCK), F32),
        ),
        in_specs=[VMEM, VMEM, SMEM, SMEM, VMEM],
        out_specs=(VMEM, VMEM),
        name="plan",
    )(holders, indices, cached, state, names)


def pack_kernel(slot, *refs):
    blocks = refs[1 : 1 + slot]
    state_ref = refs[1 + slot]
    out_ref = refs[2 + slot]
    for s in range(slot):
        out_ref[0, s * BLOCK : (s + 1) * BLOCK, :] = blocks[s][0]
    base = slot * BLOCK
    width = out_ref.shape[2]
    groups = width // LANES
    rows = state_ref.shape[1] // groups
    for b in range(groups):
        out_ref[0, base : base + rows, b * LANES : (b + 1) * LANES] = state_ref[
            0, b * rows : (b + 1) * rows, :
        ]


def pack(asked, block_pool, states):
    peers = asked.shape[0]
    slot = asked.shape[1] - 1
    width = block_pool.shape[2]
    state_rows = states.shape[1] * LANES // width
    rows = slot * BLOCK + state_rows

    def block_spec(s):
        return pl.BlockSpec((1, BLOCK, width), lambda j, asked_ref: (asked_ref[j, s], 0, 0))

    return pl.pallas_call(
        functools.partial(pack_kernel, slot),
        out_shape=jax.ShapeDtypeStruct((peers, rows, width), BF16),
        grid_spec=pltpu.PrefetchScalarGridSpec(
            num_scalar_prefetch=1,
            grid=(peers,),
            in_specs=[block_spec(s) for s in range(slot)]
            + [pl.BlockSpec((1,) + states.shape[1:], lambda j, asked_ref: (asked_ref[j, slot], 0, 0))],
            out_specs=pl.BlockSpec((1, rows, width), lambda j, asked_ref: (j, 0, 0)),
        ),
        compiler_params=pltpu.CompilerParams(vmem_limit_bytes=8 << 20),
        name="pack",
    )(asked, *([block_pool] * slot), states)


def scan_kernel(x_ref, maps_ref, steps_ref, decays_ref, tokens_ref, sum_ref, local_ref, fade_ref, keep_ref):
    length = x_ref.shape[0]
    rows_i = lax.broadcasted_iota(jnp.int32, (length, length), 0)
    cols_i = lax.broadcasted_iota(jnp.int32, (length, length), 1)
    causal = rows_i >= cols_i
    running = jnp.dot(
        causal.astype(F32), decays_ref[...], precision=HIGH, preferred_element_type=F32
    )
    last = running[length - 1 : length, :]
    middle = 0.5 * last
    rise = jnp.exp(running - middle)
    fall = jnp.exp(middle - running) * steps_ref[...]
    half = jnp.exp(middle)
    fade_ref[...] = jnp.exp(running)
    keep_ref[...] = jnp.exp(last)
    entry = maps_ref[:, :NSTATE]
    readout = maps_ref[:, NSTATE:]
    meeting = lax.dot_general(
        readout, entry, (((1,), (1,)), ((), ())), precision=HIGH, preferred_element_type=F32
    )
    meeting = split_rows(jnp.where(causal, meeting, 0.0))
    per = LANES // NSTATE
    tiled = jnp.concatenate([entry] * per, 1)
    tiled_high = tiled.astype(BF16)
    tiled_low = (tiled - tiled_high.astype(F32)).astype(BF16)
    tiled = jnp.concatenate([tiled_high, tiled_low], 1)
    sub = lax.broadcasted_iota(jnp.int32, (LANES, LANES), 0)
    lane = lax.broadcasted_iota(jnp.int32, (LANES, LANES), 1)
    own = (sub % per) == (lane // NSTATE)
    heads_per = LANES // SSM_DIM
    state_rows = LANES // per
    for q in range(x_ref.shape[1] // LANES):
        cols = slice(q * LANES, (q + 1) * LANES)
        pair = slice(q * heads_per, (q + 1) * heads_per)
        drive = (x_ref[:, cols].astype(F32) * spread(fall[:, pair], SSM_DIM)).astype(BF16)
        both = jnp.dot(meeting, drive, preferred_element_type=F32)
        part = both[:length] + both[length:]
        sum_ref[:, cols] = tokens_ref[:, cols].astype(F32) + part * spread(rise[:, pair], SSM_DIM)
        outer = lax.dot_general(
            drive, tiled, (((0,), (0,)), ((), ())), preferred_element_type=F32
        )
        outer = jnp.where(own, outer[:, :LANES] + outer[:, LANES:], 0.0)
        folded = jnp.sum(outer.reshape(state_rows, per, LANES), axis=1)
        upper = lax.broadcasted_iota(jnp.int32, (state_rows, LANES), 0) < state_rows // 2
        scale = jnp.where(
            upper,
            jnp.broadcast_to(half[:, q * heads_per : q * heads_per + 1], (state_rows, LANES)),
            jnp.broadcast_to(half[:, q * heads_per + 1 : q * heads_per + 2], (state_rows, LANES)),
        )
        local_ref[q * state_rows : (q + 1) * state_rows, :] = folded * scale


def scan_local(x, maps, steps, decays, tokens):
    length, width = x.shape
    return pl.pallas_call(
        scan_kernel,
        out_shape=(
            jax.ShapeDtypeStruct((length, width), F32),
            jax.ShapeDtypeStruct((width * NSTATE // LANES, LANES), F32),
            jax.ShapeDtypeStruct(steps.shape, F32),
            jax.ShapeDtypeStruct((1, steps.shape[1]), F32),
        ),
        in_specs=[VMEM] * 5,
        out_specs=(VMEM,) * 4,
        compiler_params=pltpu.CompilerParams(vmem_limit_bytes=56 << 20),
        name="scan_local",
    )(x, maps, steps, decays, tokens)


def mix_kernel(
    owner_ref,
    q_ref,
    kv_ref,
    got_ref,
    known_ref,
    sum_ref,
    local_ref,
    fade_ref,
    keep_ref,
    maps_ref,
    gain_ref,
    names_ref,
    router_ref,
    mixed_out,
    normed_ref,
    send_out,
    final_ref,
    weights_ref,
    total_ref,
    mixed_ref,
    send_ref,
    mixed_sem,
    send_sems,
):
    length, width = q_ref.shape
    peers = got_ref.shape[0]
    groups = HEADS // KV_HEADS
    state_rows = width * NSTATE // kv_ref.shape[1]
    block_rows = got_ref.shape[1] - state_rows
    past = peers * block_rows
    owner = owner_ref[0]
    per = LANES // NSTATE
    fold = LANES // per
    heads_per = LANES // SSM_DIM
    readout = maps_ref[:, NSTATE:]
    readout = split_rows(jnp.concatenate([readout] * per, 1))
    sub = lax.broadcasted_iota(jnp.int32, (fold, per, LANES), 1)
    lane = lax.broadcasted_iota(jnp.int32, (fold, per, LANES), 2)
    own = sub == lane // NSTATE
    fade = fade_ref[...]
    keep = keep_ref[...]
    token = lax.broadcasted_iota(jnp.int32, (length, length), 0)
    other = lax.broadcasted_iota(jnp.int32, (length, length), 1)
    seen = jnp.concatenate(
        [
            jnp.broadcast_to(known_ref[...], (length, past)),
            jnp.where(other <= token, 0.0, -1e30).astype(F32),
        ],
        1,
    )
    seen = jnp.concatenate([seen] * groups, 0)
    half = kv_ref.shape[1] // 2
    squares = jnp.zeros((length, LANES), F32)
    for g in range(KV_HEADS):
        key_cols = slice(g * HEAD, (g + 1) * HEAD)
        value_cols = slice(half + g * HEAD, half + (g + 1) * HEAD)
        keys = jnp.concatenate(
            [got_ref[j, 0:block_rows, key_cols] for j in range(peers)] + [kv_ref[:, key_cols]], 0
        )
        values = jnp.concatenate(
            [got_ref[j, 0:block_rows, value_cols] for j in range(peers)] + [kv_ref[:, value_cols]], 0
        )
        asks = jnp.concatenate(
            [
                q_ref[:, (g * groups + i) * HEAD : (g * groups + i + 1) * HEAD]
                for i in range(groups)
            ],
            0,
        )
        scores = (
            lax.dot_general(asks, keys, (((1,), (1,)), ((), ())), preferred_element_type=F32)
            + seen
        )
        top = jnp.max(scores, axis=1, keepdims=True)
        weights = jnp.exp2((scores - top) * (HEAD ** (-0.5) * math.log2(math.e)))
        attended = jnp.dot(weights.astype(BF16), values, preferred_element_type=F32)
        attended = attended * (1.0 / jnp.sum(weights, axis=1, keepdims=True))
        for i in range(groups):
            q = g * groups + i
            cols = slice(q * LANES, (q + 1) * LANES)
            per_side = state_rows // fold
            rows_at = block_rows + (q % per_side) * fold
            start = got_ref[
                owner, rows_at : rows_at + fold, (q // per_side) * LANES : (q // per_side + 1) * LANES
            ].astype(F32)
            wide = jnp.where(own, jnp.broadcast_to(start[:, None, :], (fold, per, LANES)), 0.0)
            wide = wide.reshape(LANES, LANES).astype(BF16)
            both = lax.dot_general(
                readout, wide, (((1,), (1,)), ((), ())), preferred_element_type=F32
            )
            pair = slice(q * heads_per, (q + 1) * heads_per)
            carried = (both[:length] + both[length:]) * spread(fade[:, pair], SSM_DIM)
            upper = lax.broadcasted_iota(jnp.int32, (fold, LANES), 0) < fold // 2
            scale = jnp.where(
                upper,
                jnp.broadcast_to(keep[:, q * heads_per : q * heads_per + 1], (fold, LANES)),
                jnp.broadcast_to(keep[:, q * heads_per + 1 : q * heads_per + 2], (fold, LANES)),
            )
            final_ref[q * fold : (q + 1) * fold, :] = (
                scale * start + local_ref[q * fold : (q + 1) * fold, :]
            )
            mixed = (sum_ref[:, cols] + attended[i * length : (i + 1) * length] + carried).astype(BF16)
            mixed_ref[:, cols] = mixed
            mixed = mixed.astype(F32)
            total_ref[:, cols] = mixed
            squares = squares + mixed * mixed
    mixed_copy = pltpu.make_async_copy(mixed_ref, mixed_out, mixed_sem)
    mixed_copy.start()
    send_copies = []
    mean = jnp.sum(squares, axis=1, keepdims=True) * (1.0 / width)
    scale = lax.rsqrt(mean + 1e-05)
    experts = router_ref.shape[0]
    hots = hots_of(names_ref[:, : 2 * length], 2 * length // experts)
    pick = (hots[0] + hots[1]).astype(BF16)
    logits = jnp.zeros((length, experts), F32)
    step = 4 * LANES
    for q in range(width // step):
        cols = slice(q * step, (q + 1) * step)
        normed = (total_ref[:, cols] * scale * gain_ref[:, cols]).astype(BF16)
        normed_ref[:, cols] = normed
        send_ref[:, cols] = lax.dot_general(
            pick, normed, (((0,), (0,)), ((), ())), preferred_element_type=F32
        ).astype(BF16)
        send_copies.append(
            pltpu.make_async_copy(send_ref.at[:, cols], send_out.at[:, cols], send_sems.at[q])
        )
        send_copies[-1].start()
        logits = logits + lax.dot_general(
            normed, router_ref[:, cols], (((1,), (1,)), ((), ())), preferred_element_type=F32
        )
    weights_ref[...] = weights_of(logits, hots)
    mixed_copy.wait()
    for copy in send_copies:
        copy.wait()


def mix(owner, *arrays):
    queries, local = arrays[0], arrays[5]
    length, width = queries.shape
    count = 2 * length
    anywhere = pl.BlockSpec(memory_space=pl.ANY)
    return pl.pallas_call(
        mix_kernel,
        out_shape=(
            pltpu.HBM((length, width), BF16),
            jax.ShapeDtypeStruct((length, width), BF16),
            pltpu.HBM((count, width), BF16),
            jax.ShapeDtypeStruct(local.shape, F32),
            jax.ShapeDtypeStruct((2 * length, count), BF16),
        ),
        in_specs=[SMEM] + [VMEM] * len(arrays),
        out_specs=(anywhere, VMEM, anywhere, VMEM, VMEM),
        scratch_shapes=[
            pltpu.VMEM((length, width), F32),
            pltpu.VMEM((length, width), BF16),
            pltpu.VMEM((count, width), BF16),
            pltpu.SemaphoreType.DMA,
            pltpu.SemaphoreType.DMA((width // (4 * LANES),)),
        ],
        compiler_params=pltpu.CompilerParams(vmem_limit_bytes=56 << 20),
        name="mix",
    )(owner, *arrays[:2], resident(arrays[2]), *arrays[3:])


def resident(array):
    return pltpu.with_memory_space_constraint(array, pltpu.VMEM)


def stream_kernel(body, arrays, chunks, *refs):
    held, fixed, out_ref = refs[:arrays], refs[arrays:-1], refs[-1]
    step = out_ref.shape[1] // chunks
    constants = [ref[...] for ref in fixed]
    for c in range(chunks):
        cols = slice(c * step, (c + 1) * step)
        out_ref[:, cols] = body([ref[:, cols] for ref in held], *constants)


def stream(body, arrays, consts, rows, chunks=4, keep=True, dtype=BF16):
    width = arrays[0].shape[1]
    moved = sum(array.shape[0] for array in arrays) + rows
    shape = (rows, width)
    return pl.pallas_call(
        functools.partial(stream_kernel, body, len(arrays), chunks),
        out_shape=pltpu.VMEM(shape, dtype) if keep else jax.ShapeDtypeStruct(shape, dtype),
        in_specs=[VMEM] * (len(arrays) + len(consts)),
        out_specs=VMEM,
        cost_estimate=pl.CostEstimate(
            flops=2 * moved * width, bytes_accessed=2 * moved * width, transcendentals=0
        ),
        compiler_params=pltpu.CompilerParams(vmem_limit_bytes=8 << 20),
    )(*[resident(array) for array in arrays], *consts)


def choose_kernel(source_ref, rows_ref, names_ref, router_ref, send_ref, weights_ref):
    experts = router_ref.shape[0]
    length, width = rows_ref.shape
    names = names_ref[pl.ds(source_ref[0], 1), :][:, : 2 * length]
    hots = hots_of(names, 2 * length // experts)
    pick = (hots[0] + hots[1]).astype(BF16)
    logits = jnp.zeros((length, experts), F32)
    step = 8 * LANES
    for q in range(width // step):
        cols = slice(q * step, (q + 1) * step)
        rows = rows_ref[:, cols]
        send_ref[:, cols] = lax.dot_general(
            pick, rows, (((0,), (0,)), ((), ())), preferred_element_type=F32
        ).astype(BF16)
        logits = logits + lax.dot_general(
            rows, router_ref[:, cols], (((1,), (1,)), ((), ())), preferred_element_type=F32
        )
    weights_ref[...] = weights_of(logits, hots)


def choose(source, rows, names, router):
    length, width = rows.shape
    return pl.pallas_call(
        choose_kernel,
        out_shape=(
            pltpu.HBM((2 * length, width), BF16),
            jax.ShapeDtypeStruct((2 * length, 2 * length), BF16),
        ),
        in_specs=[SMEM] + [VMEM] * 3,
        out_specs=(VMEM, VMEM),
        compiler_params=pltpu.CompilerParams(vmem_limit_bytes=8 << 20),
        name="choose",
    )(source, resident(rows), names, router)


def weighed(parts, weights):
    both = jnp.dot(weights, parts, preferred_element_type=F32)
    length = weights.shape[0] // 2
    return both[:length] + both[length:]


def combine(parts, weights):
    def body(held, weights):
        return weighed(held[0], weights).astype(BF16)

    return stream(body, [parts], [weights], weights.shape[0] // 2)


def held_kernel(body, arrays, *refs):
    held, far_ref, out_ref = refs[:arrays], refs[arrays], refs[arrays + 1]
    near_ref, made_ref, sem, out_sems = refs[arrays + 2 :]
    chunks = out_sems.shape[0]
    step = out_ref.shape[1] // chunks
    copy = pltpu.make_async_copy(far_ref, near_ref, sem)
    copy.start()
    outs = []
    for c in range(chunks):
        cols = slice(c * step, (c + 1) * step)
        made = body(cols, *held)
        if c == 0:
            copy.wait()
        made_ref[:, cols] = (made + near_ref[:, cols].astype(F32)).astype(BF16)
        outs.append(
            pltpu.make_async_copy(made_ref.at[:, cols], out_ref.at[:, cols], out_sems.at[c])
        )
        outs[-1].start()
    for out in outs:
        out.wait()


def held_call(body, arrays, far, chunks=4):
    anywhere = pl.BlockSpec(memory_space=pl.ANY)
    return pl.pallas_call(
        functools.partial(held_kernel, body, len(arrays)),
        out_shape=pltpu.HBM(far.shape, BF16),
        in_specs=[VMEM] * len(arrays) + [anywhere],
        out_specs=anywhere,
        scratch_shapes=[
            pltpu.VMEM(far.shape, BF16),
            pltpu.VMEM(far.shape, BF16),
            pltpu.SemaphoreType.DMA,
            pltpu.SemaphoreType.DMA((chunks,)),
        ],
        compiler_params=pltpu.CompilerParams(vmem_limit_bytes=16 << 20),
    )(*[resident(array) for array in arrays], pltpu.with_memory_space_constraint(far, pltpu.HBM))


def finish(parts, weights, sums, mixed):
    def body(cols, parts_ref, weights_ref, *sums_refs):
        total = weighed(parts_ref[:, cols], weights_ref[...])
        for ref in sums_refs:
            total = total + ref[:, cols].astype(F32)
        return total

    return held_call(body, [parts, weights] + sums, mixed)


def combine_keep_kernel(parts_ref, weights_ref, far_ref, out_ref, near_ref, sem):
    copy = pltpu.make_async_copy(far_ref, near_ref, sem)
    copy.start()
    step = 8 * LANES
    for at in range(0, out_ref.shape[1], step):
        cols = slice(at, at + step)
        out_ref[:, cols] = weighed(parts_ref[:, cols], weights_ref[...]).astype(BF16)
    copy.wait()


def combine_keep(parts, weights, far):
    return pl.pallas_call(
        combine_keep_kernel,
        out_shape=(
            pltpu.VMEM((weights.shape[0] // 2, parts.shape[1]), BF16),
            pltpu.VMEM(far.shape, BF16),
        ),
        in_specs=[VMEM, VMEM, pl.BlockSpec(memory_space=pl.ANY)],
        out_specs=(VMEM, VMEM),
        scratch_shapes=[pltpu.SemaphoreType.DMA],
        compiler_params=pltpu.CompilerParams(vmem_limit_bytes=8 << 20),
        name="combine_keep",
    )(resident(parts), weights, pltpu.with_memory_space_constraint(far, pltpu.HBM))


def join(first, others):
    if not others:
        return first

    def body(held):
        return sum(part.astype(F32) for part in held).astype(BF16)

    return stream(body, [first] + others, [], first.shape[0], keep=False)


def expert_kernel(count, ups, downs, *refs):
    sources = refs[:count]
    up_hbm, down_hbm = refs[count : count + 2]
    outs = refs[count + 2 : 2 * count + 2]
    up_ref, down_ref, hidden_ref, made_ref, sems, out_sems = refs[2 * count + 2 :]
    each, _ = sources[0].shape
    copies = [
        pltpu.make_async_copy(
            hbm.at[:, pl.ds(start, size)], ref.at[:, pl.ds(start, size)], sems.at[base + n]
        )
        for hbm, ref, blocks, base in (
            (up_hbm, up_ref, ups, 0),
            (down_hbm, down_ref, downs, len(ups)),
        )
        for n, (start, size) in enumerate(blocks)
    ]
    for copy in copies:
        copy.start()
    if count == 1:
        rows = sources[0][...]
    else:
        rows = jnp.concatenate([source[...] for source in sources], 0)
    tile = 2 * LANES
    for (start, size), copy in zip(ups, copies):
        copy.wait()
        for at in range(start, start + size, tile):
            cols = slice(at, min(at + tile, start + size))
            lifted = jnp.dot(rows, up_ref[:, cols], preferred_element_type=F32)
            hidden_ref[:, cols] = (lifted / (1.0 + jnp.exp(-lifted))).astype(BF16)
    hidden = hidden_ref[...]
    tile = 4 * LANES
    flying = []
    for n, ((start, size), copy) in enumerate(zip(downs, copies[len(ups) :])):
        copy.wait()
        for at in range(start, start + size, tile):
            cols = slice(at, at + tile)
            made_ref[:, cols] = jnp.dot(
                hidden, down_ref[:, cols], preferred_element_type=F32
            ).astype(BF16)
        for k in range(count):
            cols = pl.ds(start, size)
            flying.append(
                pltpu.make_async_copy(
                    made_ref.at[pl.ds(k * each, each), cols],
                    outs[k].at[:, cols],
                    out_sems.at[k, n],
                )
            )
            flying[-1].start()
    for copy in flying:
        copy.wait()


def blocks_of(total, shares):
    unit = total // sum(shares)
    if unit % LANES or unit * sum(shares) != total:
        return [(0, total)]
    ends = [unit * sum(shares[: n + 1]) for n in range(len(shares))]
    return [(end - unit * share, unit * share) for end, share in zip(ends, shares)]


def apply_expert(chunks, up_local, down_local):
    count = len(chunks)
    each, width = chunks[0].shape
    hidden = up_local.shape[1]
    anywhere = pl.BlockSpec(memory_space=pl.ANY)
    ups = blocks_of(hidden, UP_SHARES)
    downs = blocks_of(width, DOWN_SHARES)
    return pl.pallas_call(
        functools.partial(expert_kernel, count, ups, downs),
        out_shape=[pltpu.HBM((each, width), BF16)] * count,
        in_specs=[VMEM] * count + [anywhere] * 2,
        out_specs=[anywhere] * count,
        scratch_shapes=[
            pltpu.VMEM(up_local.shape, BF16),
            pltpu.VMEM(down_local.shape, BF16),
            pltpu.VMEM((count * each, hidden), BF16),
            pltpu.VMEM((count * each, width), BF16),
            pltpu.SemaphoreType.DMA((len(ups) + len(downs),)),
            pltpu.SemaphoreType.DMA((count, len(downs))),
        ],
        cost_estimate=pl.CostEstimate(
            flops=4 * count * each * width * hidden,
            bytes_accessed=4 * width * hidden + 4 * count * each * width,
            transcendentals=count * each * hidden,
        ),
        compiler_params=pltpu.CompilerParams(vmem_limit_bytes=50 << 20),
        name="expert",
    )(
        *[resident(chunk) for chunk in chunks],
        pltpu.with_memory_space_constraint(up_local, pltpu.HBM),
        pltpu.with_memory_space_constraint(down_local, pltpu.HBM),
    )


def local(
    tokens,
    queries,
    keys_values,
    scan_input,
    state_maps,
    step_size,
    step_decay,
    block_pool,
    state_pool,
    block_holder,
    block_index,
    cached_blocks,
    state_holder,
    state_index,
    norm_gain,
    router_weight,
    expert_ids,
    up_weight,
    down_weight,
):
    peers = lax.axis_size("dp")
    columns = lax.axis_size("expert")
    near = peers // 2

    def route(turn, side):
        return [
            (h * near + i, (h + side) % 2 * near + (i + turn) % near)
            for h in range(2)
            for i in range(near)
        ]

    def move(rows, turn, side):
        return lax.ppermute(rows, "dp", route(turn, side))

    def swap_rows(rows):
        blocks = rows.reshape(columns, -1, rows.shape[-1])
        moved = lax.all_to_all(blocks, "expert", split_axis=0, concat_axis=0, tiled=True)
        return moved.reshape(rows.shape)

    slot = block_holder.shape[1] // peers
    count = 2 * expert_ids.shape[0]
    ask, known = plan(peers, block_holder, block_index, cached_blocks, state_index, expert_ids.T)
    asked = lax.all_to_all(ask, "dp", split_axis=0, concat_axis=0, tiled=True)[:, 0]
    place = lax.axis_index("dp")

    def source_of(turn):
        return (place // near + 1) % 2 * near + (place % near + near - turn) % near

    states = state_pool.reshape(state_pool.shape[0], -1, LANES).astype(BF16)
    packed = pack(asked[:, count : count + slot + 1], block_pool, states)
    got = lax.all_to_all(packed, "dp", split_axis=0, concat_axis=0, tiled=True)

    router = router_weight.T
    sums, from_inputs, fade, keep = scan_local(
        scan_input, state_maps, step_size, step_decay, tokens
    )
    mixed, normed, send, final_state, weights = mix(
        state_holder, queries, keys_values, got, known, sums, from_inputs, fade, keep, state_maps,
        norm_gain[None, :], ask[0], router,
    )
    up_local, down_local = up_weight[0], down_weight[0]

    far_rows = [move(normed, 0, 1)]
    near_in = swap_rows(send)
    near_moved = [move(near_in, turn, 0) for turn in range(1, near)]
    far_rows += [move(far_rows[0], turn, 0) for turn in range(1, near)]
    far_in, far_weights = [], []
    for turn in range(near):
        chosen, gates = choose(source_of(turn)[None], far_rows[turn], asked, router)
        far_in.append(swap_rows(chosen))
        far_weights.append(gates)

    def experts_on(rows):
        return list(apply_expert(rows, up_local, down_local))

    near_out, first_out = experts_on([near_in, far_in[0]])
    moved_out, far_out = [], [first_out]
    if near > 1:
        late = experts_on(near_moved + far_in[1:])
        moved_out, far_out = late[: near - 1], far_out + late[near - 1 :]

    far_sums = []
    for turn in range(near):
        back = swap_rows(far_out[turn])
        if turn > 0 and turn == near - 1:
            part, near_out = combine_keep(back, far_weights[turn], near_out)
        else:
            part = combine(back, far_weights[turn])
        far_sums.append(move(part, near - turn, 1))
    moved_back = [move(rows, near - turn, 0) for turn, rows in enumerate(moved_out, 1)]
    joined = join(near_out, moved_back)
    near_back = swap_rows(joined)
    layer_out = finish(near_back, weights, far_sums, mixed)
    return (layer_out, final_state.reshape(1, -1))


def solution(mesh):
    placed = (
        P(("dp", "expert"), None),
        P(("dp", "expert"), None),
        P(("dp", "expert"), None),
        P(("dp", "expert"), None),
        P(("dp", "expert"), None),
        P(("dp", "expert"), None),
        P(("dp", "expert"), None),
        P(("dp", "expert"), None, None),
        P(("dp", "expert"), None),
        P(("dp", "expert"), None),
        P(("dp", "expert"), None),
        P(("dp", "expert")),
        P(("dp", "expert")),
        P(("dp", "expert")),
        P(),
        P(),
        P(("dp", "expert"), None),
        P("expert", None, "dp"),
        P("expert", "dp", None),
    )
    return jax.shard_map(
        local,
        mesh=mesh,
        in_specs=placed,
        out_specs=(P(("dp", "expert"), None), P(("dp", "expert"), None)),
        check_vma=False,
    )
```

```python
import functools
import math

import jax
import jax.numpy as jnp
from jax import lax
from jax.experimental import pallas as pl
from jax.experimental.pallas import tpu as pltpu
from jax.sharding import PartitionSpec as P


HEADS = 32
KV_HEADS = 8
HEAD = 128
SSM_DIM = 64
NSTATE = 16
BLOCK = 16
LANES = 128
UP_SHARES = (1, 2, 2, 2)
DOWN_SHARES = (4, 2, 1, 1)
HIGH = lax.Precision.HIGHEST
F32 = jnp.float32
BF16 = jnp.bfloat16
VMEM = pl.BlockSpec(memory_space=pltpu.VMEM)
SMEM = pl.BlockSpec(memory_space=pltpu.SMEM)


def split_rows(value):
    high = value.astype(BF16)
    low = (value - high.astype(F32)).astype(BF16)
    return jnp.concatenate([high, low], 0)


def spread(column_pair, width):
    rows = column_pair.shape[0]
    lane = lax.broadcasted_iota(jnp.int32, (rows, LANES), 1)
    return jnp.where(
        lane < width,
        jnp.broadcast_to(column_pair[:, 0:1], (rows, LANES)),
        jnp.broadcast_to(column_pair[:, 1:2], (rows, LANES)),
    )


def places_of(names):
    count = names.shape[1]
    length = count // 2
    token = lax.broadcasted_iota(jnp.int32, (length, count), 0)
    lane = lax.broadcasted_iota(jnp.int32, (length, count), 1)
    wide = jnp.broadcast_to(names.astype(F32), (length, count))
    return [
        jnp.sum(jnp.where(lane == 2 * token + j, wide, 0.0), axis=1, keepdims=True)
        for j in range(2)
    ]


def hots_of(names, capacity):
    columns = places_of(names)
    count = names.shape[1]
    length = count // 2
    lane = lax.broadcasted_iota(jnp.int32, (length, count), 1)
    expert = (lane // capacity).astype(F32)
    place = (lane % capacity).astype(F32)
    ones = [jnp.where(expert == column, 1.0, 0.0) for column in columns]
    rows = lax.broadcasted_iota(jnp.int32, (length, length), 0)
    cols = lax.broadcasted_iota(jnp.int32, (length, length), 1)
    earlier = jnp.where(rows > cols, 1.0, 0.0).astype(BF16)
    before = jnp.dot(earlier, (ones[0] + ones[1]).astype(BF16), preferred_element_type=F32)
    here = jnp.where(before == place, 1.0, 0.0)
    return [one * here for one in ones]


def weights_of(logits, hots):
    experts = logits.shape[1]
    count = hots[0].shape[1]
    sub = lax.broadcasted_iota(jnp.int32, (experts, count), 0)
    lane = lax.broadcasted_iota(jnp.int32, (experts, count), 1)
    wider = jnp.where(lane // (count // experts) == sub, 1.0, 0.0)
    wide = jnp.dot(logits, wider, precision=HIGH, preferred_element_type=F32)
    lifted = [
        lax.logistic(jnp.sum(wide * hot, axis=1, keepdims=True)) for hot in hots
    ]
    total = lifted[0] + lifted[1]
    weights = sum(hot * (lift / total) for hot, lift in zip(hots, lifted))
    return split_rows(weights)


def turned(row):
    count = row.shape[1]
    sub = lax.broadcasted_iota(jnp.int32, (count, count), 0)
    lane = lax.broadcasted_iota(jnp.int32, (count, count), 1)
    return jnp.sum(
        jnp.where(sub == lane, jnp.broadcast_to(row, (count, count)), 0.0), axis=1, keepdims=True
    )


def plan_kernel(slot, holders_ref, indices_ref, cached_ref, state_ref, names_ref, ask_ref, known_ref):
    peers = ask_ref.shape[0]
    entries = holders_ref.shape[1]
    holders = holders_ref[...].astype(F32)
    square = (entries, entries)
    sub = lax.broadcasted_iota(jnp.int32, square, 0)
    lane = lax.broadcasted_iota(jnp.int32, square, 1)
    same = jnp.where(
        (turned(holders) == jnp.broadcast_to(holders, square)) & (sub < lane), 1.0, 0.0
    )
    seats = turned(holders * slot + jnp.sum(same, axis=0, keepdims=True))
    indices = turned(indices_ref[...].astype(F32))
    length = names_ref.shape[1]
    count = 2 * length
    names = [turned(names_ref[j : j + 1, :].astype(F32)) for j in range(2)]
    token = lax.broadcasted_iota(jnp.int32, (length, count), 0)
    at = lax.broadcasted_iota(jnp.int32, (length, count), 1)
    laid = sum(
        jnp.where(at == 2 * token + j, jnp.broadcast_to(names[j], (length, count)), 0.0)
        for j in range(2)
    )
    laid = jnp.sum(laid, axis=0, keepdims=True)
    spots = lax.broadcasted_iota(jnp.int32, (entries, LANES), 1)
    wide = jnp.broadcast_to(indices, (entries, LANES))
    for j in range(peers):
        here = (seats == (spots + j * slot).astype(F32)) & (spots < slot)
        asks = jnp.sum(jnp.where(here, wide, 0.0), axis=0, keepdims=True)
        asks = jnp.where(spots[:1] == slot, state_ref[0].astype(F32), asks)
        ask_ref[j, 0:1, :] = jnp.concatenate([laid, asks], 1).astype(jnp.int32)
    past = known_ref.shape[1]
    spots = lax.broadcasted_iota(jnp.int32, (entries, past), 1) // BLOCK
    order = lax.broadcasted_iota(jnp.int32, (entries, past), 0).astype(F32)
    entry = jnp.sum(
        jnp.where(seats == spots.astype(F32), order, 0.0), axis=0, keepdims=True
    )
    known_ref[...] = jnp.where(entry < cached_ref[0].astype(F32), 0.0, -1e30)


def plan(peers, holders, indices, cached, state, names):
    entries = holders.shape[1]
    return pl.pallas_call(
        functools.partial(plan_kernel, entries // peers),
        out_shape=(
            jax.ShapeDtypeStruct((peers, 1, 2 * names.shape[1] + LANES), jnp.int32),
            jax.ShapeDtypeStruct((1, entries * BLOCK), F32),
        ),
        in_specs=[VMEM, VMEM, SMEM, SMEM, VMEM],
        out_specs=(VMEM, VMEM),
        name="plan",
    )(holders, indices, cached, state, names)


def pack_kernel(slot, *refs):
    blocks = refs[1 : 1 + slot]
    state_ref = refs[1 + slot]
    out_ref = refs[2 + slot]
    for s in range(slot):
        out_ref[0, s * BLOCK : (s + 1) * BLOCK, :] = blocks[s][0]
    base = slot * BLOCK
    width = out_ref.shape[2]
    groups = width // LANES
    rows = state_ref.shape[1] // groups
    for b in range(groups):
        out_ref[0, base : base + rows, b * LANES : (b + 1) * LANES] = state_ref[
            0, b * rows : (b + 1) * rows, :
        ]


def pack(asked, block_pool, states):
    peers = asked.shape[0]
    slot = asked.shape[1] - 1
    width = block_pool.shape[2]
    state_rows = states.shape[1] * LANES // width
    rows = slot * BLOCK + state_rows

    def block_spec(s):
        return pl.BlockSpec((1, BLOCK, width), lambda j, asked_ref: (asked_ref[j, s], 0, 0))

    return pl.pallas_call(
        functools.partial(pack_kernel, slot),
        out_shape=jax.ShapeDtypeStruct((peers, rows, width), BF16),
        grid_spec=pltpu.PrefetchScalarGridSpec(
            num_scalar_prefetch=1,
            grid=(peers,),
            in_specs=[block_spec(s) for s in range(slot)]
            + [pl.BlockSpec((1,) + states.shape[1:], lambda j, asked_ref: (asked_ref[j, slot], 0, 0))],
            out_specs=pl.BlockSpec((1, rows, width), lambda j, asked_ref: (j, 0, 0)),
        ),
        compiler_params=pltpu.CompilerParams(vmem_limit_bytes=8 << 20),
        name="pack",
    )(asked, *([block_pool] * slot), states)


def scan_kernel(x_ref, maps_ref, steps_ref, decays_ref, tokens_ref, sum_ref, local_ref, fade_ref, keep_ref):
    length = x_ref.shape[0]
    rows_i = lax.broadcasted_iota(jnp.int32, (length, length), 0)
    cols_i = lax.broadcasted_iota(jnp.int32, (length, length), 1)
    causal = rows_i >= cols_i
    running = jnp.dot(
        causal.astype(F32), decays_ref[...], precision=HIGH, preferred_element_type=F32
    )
    last = running[length - 1 : length, :]
    middle = 0.5 * last
    rise = jnp.exp(running - middle)
    fall = jnp.exp(middle - running) * steps_ref[...]
    half = jnp.exp(middle)
    fade_ref[...] = jnp.exp(running)
    keep_ref[...] = jnp.exp(last)
    entry = maps_ref[:, :NSTATE]
    readout = maps_ref[:, NSTATE:]
    meeting = lax.dot_general(
        readout, entry, (((1,), (1,)), ((), ())), precision=HIGH, preferred_element_type=F32
    )
    meeting = split_rows(jnp.where(causal, meeting, 0.0))
    per = LANES // NSTATE
    tiled = jnp.concatenate([entry] * per, 1)
    tiled_high = tiled.astype(BF16)
    tiled_low = (tiled - tiled_high.astype(F32)).astype(BF16)
    tiled = jnp.concatenate([tiled_high, tiled_low], 1)
    sub = lax.broadcasted_iota(jnp.int32, (LANES, LANES), 0)
    lane = lax.broadcasted_iota(jnp.int32, (LANES, LANES), 1)
    own = (sub % per) == (lane // NSTATE)
    heads_per = LANES // SSM_DIM
    state_rows = LANES // per
    for q in range(x_ref.shape[1] // LANES):
        cols = slice(q * LANES, (q + 1) * LANES)
        pair = slice(q * heads_per, (q + 1) * heads_per)
        drive = (x_ref[:, cols].astype(F32) * spread(fall[:, pair], SSM_DIM)).astype(BF16)
        both = jnp.dot(meeting, drive, preferred_element_type=F32)
        part = both[:length] + both[length:]
        sum_ref[:, cols] = tokens_ref[:, cols].astype(F32) + part * spread(rise[:, pair], SSM_DIM)
        outer = lax.dot_general(
            drive, tiled, (((0,), (0,)), ((), ())), preferred_element_type=F32
        )
        outer = jnp.where(own, outer[:, :LANES] + outer[:, LANES:], 0.0)
        folded = jnp.sum(outer.reshape(state_rows, per, LANES), axis=1)
        upper = lax.broadcasted_iota(jnp.int32, (state_rows, LANES), 0) < state_rows // 2
        scale = jnp.where(
            upper,
            jnp.broadcast_to(half[:, q * heads_per : q * heads_per + 1], (state_rows, LANES)),
            jnp.broadcast_to(half[:, q * heads_per + 1 : q * heads_per + 2], (state_rows, LANES)),
        )
        local_ref[q * state_rows : (q + 1) * state_rows, :] = folded * scale


def scan_local(x, maps, steps, decays, tokens):
    length, width = x.shape
    return pl.pallas_call(
        scan_kernel,
        out_shape=(
            jax.ShapeDtypeStruct((length, width), F32),
            jax.ShapeDtypeStruct((width * NSTATE // LANES, LANES), F32),
            jax.ShapeDtypeStruct(steps.shape, F32),
            jax.ShapeDtypeStruct((1, steps.shape[1]), F32),
        ),
        in_specs=[VMEM] * 5,
        out_specs=(VMEM,) * 4,
        compiler_params=pltpu.CompilerParams(vmem_limit_bytes=56 << 20),
        name="scan_local",
    )(x, maps, steps, decays, tokens)


def mix_kernel(
    owner_ref,
    q_ref,
    kv_ref,
    got_ref,
    known_ref,
    sum_ref,
    local_ref,
    fade_ref,
    keep_ref,
    maps_ref,
    gain_ref,
    pick_ref,
    mixed_out,
    normed_ref,
    send_out,
    final_ref,
    total_ref,
    mixed_ref,
    send_ref,
    mixed_sem,
    send_sems,
):
    length, width = q_ref.shape
    peers = got_ref.shape[0]
    groups = HEADS // KV_HEADS
    state_rows = width * NSTATE // kv_ref.shape[1]
    block_rows = got_ref.shape[1] - state_rows
    past = peers * block_rows
    owner = owner_ref[0]
    per = LANES // NSTATE
    fold = LANES // per
    heads_per = LANES // SSM_DIM
    readout = maps_ref[:, NSTATE:]
    readout = split_rows(jnp.concatenate([readout] * per, 1))
    sub = lax.broadcasted_iota(jnp.int32, (fold, per, LANES), 1)
    lane = lax.broadcasted_iota(jnp.int32, (fold, per, LANES), 2)
    own = sub == lane // NSTATE
    fade = fade_ref[...]
    keep = keep_ref[...]
    token = lax.broadcasted_iota(jnp.int32, (length, length), 0)
    other = lax.broadcasted_iota(jnp.int32, (length, length), 1)
    seen = jnp.concatenate(
        [
            jnp.broadcast_to(known_ref[...], (length, past)),
            jnp.where(other <= token, 0.0, -1e30).astype(F32),
        ],
        1,
    )
    seen = jnp.concatenate([seen] * groups, 0)
    half = kv_ref.shape[1] // 2
    squares = jnp.zeros((length, LANES), F32)
    for g in range(KV_HEADS):
        key_cols = slice(g * HEAD, (g + 1) * HEAD)
        value_cols = slice(half + g * HEAD, half + (g + 1) * HEAD)
        keys = jnp.concatenate(
            [got_ref[j, 0:block_rows, key_cols] for j in range(peers)] + [kv_ref[:, key_cols]], 0
        )
        values = jnp.concatenate(
            [got_ref[j, 0:block_rows, value_cols] for j in range(peers)] + [kv_ref[:, value_cols]], 0
        )
        asks = jnp.concatenate(
            [
                q_ref[:, (g * groups + i) * HEAD : (g * groups + i + 1) * HEAD]
                for i in range(groups)
            ],
            0,
        )
        scores = (
            lax.dot_general(asks, keys, (((1,), (1,)), ((), ())), preferred_element_type=F32)
            + seen
        )
        top = jnp.max(scores, axis=1, keepdims=True)
        weights = jnp.exp2((scores - top) * (HEAD ** (-0.5) * math.log2(math.e)))
        attended = jnp.dot(weights.astype(BF16), values, preferred_element_type=F32)
        attended = attended * (1.0 / jnp.sum(weights, axis=1, keepdims=True))
        for i in range(groups):
            q = g * groups + i
            cols = slice(q * LANES, (q + 1) * LANES)
            per_side = state_rows // fold
            rows_at = block_rows + (q % per_side) * fold
            start = got_ref[
                owner, rows_at : rows_at + fold, (q // per_side) * LANES : (q // per_side + 1) * LANES
            ].astype(F32)
            wide = jnp.where(own, jnp.broadcast_to(start[:, None, :], (fold, per, LANES)), 0.0)
            wide = wide.reshape(LANES, LANES).astype(BF16)
            both = lax.dot_general(
                readout, wide, (((1,), (1,)), ((), ())), preferred_element_type=F32
            )
            pair = slice(q * heads_per, (q + 1) * heads_per)
            carried = (both[:length] + both[length:]) * spread(fade[:, pair], SSM_DIM)
            upper = lax.broadcasted_iota(jnp.int32, (fold, LANES), 0) < fold // 2
            scale = jnp.where(
                upper,
                jnp.broadcast_to(keep[:, q * heads_per : q * heads_per + 1], (fold, LANES)),
                jnp.broadcast_to(keep[:, q * heads_per + 1 : q * heads_per + 2], (fold, LANES)),
            )
            final_ref[q * fold : (q + 1) * fold, :] = (
                scale * start + local_ref[q * fold : (q + 1) * fold, :]
            )
            mixed = (sum_ref[:, cols] + attended[i * length : (i + 1) * length] + carried).astype(BF16)
            mixed_ref[:, cols] = mixed
            mixed = mixed.astype(F32)
            total_ref[:, cols] = mixed
            squares = squares + mixed * mixed
    mixed_copy = pltpu.make_async_copy(mixed_ref, mixed_out, mixed_sem)
    mixed_copy.start()
    send_copies = []
    mean = jnp.sum(squares, axis=1, keepdims=True) * (1.0 / width)
    scale = lax.rsqrt(mean + 1e-05)
    pick = pick_ref[...]
    step = 4 * LANES
    for q in range(width // step):
        cols = slice(q * step, (q + 1) * step)
        normed = (total_ref[:, cols] * scale * gain_ref[:, cols]).astype(BF16)
        normed_ref[:, cols] = normed
        send_ref[:, cols] = lax.dot_general(
            pick, normed, (((0,), (0,)), ((), ())), preferred_element_type=F32
        ).astype(BF16)
        send_copies.append(
            pltpu.make_async_copy(send_ref.at[:, cols], send_out.at[:, cols], send_sems.at[q])
        )
        send_copies[-1].start()
    mixed_copy.wait()
    for copy in send_copies:
        copy.wait()


def mix(owner, *arrays):
    queries, local = arrays[0], arrays[5]
    length, width = queries.shape
    count = 2 * length
    anywhere = pl.BlockSpec(memory_space=pl.ANY)
    return pl.pallas_call(
        mix_kernel,
        out_shape=(
            pltpu.HBM((length, width), BF16),
            jax.ShapeDtypeStruct((length, width), BF16),
            pltpu.HBM((count, width), BF16),
            jax.ShapeDtypeStruct(local.shape, F32),
        ),
        in_specs=[SMEM] + [VMEM] * len(arrays),
        out_specs=(anywhere, VMEM, anywhere, VMEM),
        scratch_shapes=[
            pltpu.VMEM((length, width), F32),
            pltpu.VMEM((length, width), BF16),
            pltpu.VMEM((count, width), BF16),
            pltpu.SemaphoreType.DMA,
            pltpu.SemaphoreType.DMA((width // (4 * LANES),)),
        ],
        compiler_params=pltpu.CompilerParams(vmem_limit_bytes=56 << 20),
        name="mix",
    )(owner, *arrays[:2], resident(arrays[2]), *arrays[3:])


def resident(array):
    return pltpu.with_memory_space_constraint(array, pltpu.VMEM)


def stream_kernel(body, arrays, chunks, *refs):
    held, fixed, out_ref = refs[:arrays], refs[arrays:-1], refs[-1]
    step = out_ref.shape[1] // chunks
    constants = [ref[...] for ref in fixed]
    for c in range(chunks):
        cols = slice(c * step, (c + 1) * step)
        out_ref[:, cols] = body([ref[:, cols] for ref in held], *constants)


def stream(body, arrays, consts, rows, chunks=4, keep=True, dtype=BF16):
    width = arrays[0].shape[1]
    moved = sum(array.shape[0] for array in arrays) + rows
    shape = (rows, width)
    return pl.pallas_call(
        functools.partial(stream_kernel, body, len(arrays), chunks),
        out_shape=pltpu.VMEM(shape, dtype) if keep else jax.ShapeDtypeStruct(shape, dtype),
        in_specs=[VMEM] * (len(arrays) + len(consts)),
        out_specs=VMEM,
        cost_estimate=pl.CostEstimate(
            flops=2 * moved * width, bytes_accessed=2 * moved * width, transcendentals=0
        ),
        compiler_params=pltpu.CompilerParams(vmem_limit_bytes=8 << 20),
    )(*[resident(array) for array in arrays], *consts)


def choose_kernel(source_ref, rows_ref, names_ref, router_ref, send_ref, weights_ref):
    experts = router_ref.shape[0]
    length, width = rows_ref.shape
    names = names_ref[pl.ds(source_ref[0], 1), :][:, : 2 * length]
    hots = hots_of(names, 2 * length // experts)
    pick = (hots[0] + hots[1]).astype(BF16)
    logits = jnp.zeros((length, experts), F32)
    step = 8 * LANES
    for q in range(width // step):
        cols = slice(q * step, (q + 1) * step)
        rows = rows_ref[:, cols]
        send_ref[:, cols] = lax.dot_general(
            pick, rows, (((0,), (0,)), ((), ())), preferred_element_type=F32
        ).astype(BF16)
        logits = logits + lax.dot_general(
            rows, router_ref[:, cols], (((1,), (1,)), ((), ())), preferred_element_type=F32
        )
    weights_ref[...] = weights_of(logits, hots)


def choose(source, rows, names, router):
    length, width = rows.shape
    return pl.pallas_call(
        choose_kernel,
        out_shape=(
            pltpu.HBM((2 * length, width), BF16),
            jax.ShapeDtypeStruct((2 * length, 2 * length), BF16),
        ),
        in_specs=[SMEM] + [VMEM] * 3,
        out_specs=(VMEM, VMEM),
        compiler_params=pltpu.CompilerParams(vmem_limit_bytes=8 << 20),
        name="choose",
    )(source, resident(rows), names, router)


def picks(sources, names, length, experts):
    number = sources.shape[0]

    def kernel(sources_ref, names_ref, *outs):
        for k, out_ref in enumerate(outs):
            names = names_ref[pl.ds(sources_ref[k], 1), :][:, : 2 * length]
            hots = hots_of(names, 2 * length // experts)
            out_ref[...] = (hots[0] + hots[1]).astype(BF16)

    return pl.pallas_call(
        kernel,
        out_shape=[jax.ShapeDtypeStruct((length, 2 * length), BF16)] * number,
        in_specs=[SMEM, VMEM],
        out_specs=[VMEM] * number,
        compiler_params=pltpu.CompilerParams(vmem_limit_bytes=56 << 20),
        name="picks",
    )(sources, names)


def gates_kernel(source_ref, rows_ref, names_ref, router_ref, weights_ref):
    length = rows_ref.shape[0]
    names = names_ref[pl.ds(source_ref[0], 1), :][:, : 2 * length]
    hots = hots_of(names, 2 * length // router_ref.shape[0])
    logits = lax.dot_general(
        rows_ref[...], router_ref[...], (((1,), (1,)), ((), ())), preferred_element_type=F32
    )
    weights_ref[...] = weights_of(logits, hots)


def gates(source, rows, names, router):
    length = rows.shape[0]
    return pl.pallas_call(
        gates_kernel,
        out_shape=jax.ShapeDtypeStruct((2 * length, 2 * length), BF16),
        in_specs=[SMEM] + [VMEM] * 3,
        out_specs=VMEM,
        compiler_params=pltpu.CompilerParams(vmem_limit_bytes=56 << 20),
        name="gates",
    )(source, rows, names, router)


def weighed(parts, weights):
    both = jnp.dot(weights, parts, preferred_element_type=F32)
    length = weights.shape[0] // 2
    return both[:length] + both[length:]


def combine(parts, weights):
    def body(held, weights):
        return weighed(held[0], weights).astype(BF16)

    return stream(body, [parts], [weights], weights.shape[0] // 2)


def held_kernel(body, arrays, *refs):
    held, far_ref, out_ref = refs[:arrays], refs[arrays], refs[arrays + 1]
    near_ref, made_ref, sem, out_sems = refs[arrays + 2 :]
    chunks = out_sems.shape[0]
    step = out_ref.shape[1] // chunks
    copy = pltpu.make_async_copy(far_ref, near_ref, sem)
    copy.start()
    outs = []
    for c in range(chunks):
        cols = slice(c * step, (c + 1) * step)
        made = body(cols, *held)
        if c == 0:
            copy.wait()
        made_ref[:, cols] = (made + near_ref[:, cols].astype(F32)).astype(BF16)
        outs.append(
            pltpu.make_async_copy(made_ref.at[:, cols], out_ref.at[:, cols], out_sems.at[c])
        )
        outs[-1].start()
    for out in outs:
        out.wait()


def held_call(body, arrays, far, chunks=4):
    anywhere = pl.BlockSpec(memory_space=pl.ANY)
    return pl.pallas_call(
        functools.partial(held_kernel, body, len(arrays)),
        out_shape=pltpu.HBM(far.shape, BF16),
        in_specs=[VMEM] * len(arrays) + [anywhere],
        out_specs=anywhere,
        scratch_shapes=[
            pltpu.VMEM(far.shape, BF16),
            pltpu.VMEM(far.shape, BF16),
            pltpu.SemaphoreType.DMA,
            pltpu.SemaphoreType.DMA((chunks,)),
        ],
        compiler_params=pltpu.CompilerParams(vmem_limit_bytes=16 << 20),
    )(*[resident(array) for array in arrays], pltpu.with_memory_space_constraint(far, pltpu.HBM))


def finish(parts, weights, sums, mixed):
    def body(cols, parts_ref, weights_ref, *sums_refs):
        total = weighed(parts_ref[:, cols], weights_ref[...])
        for ref in sums_refs:
            total = total + ref[:, cols].astype(F32)
        return total

    return held_call(body, [parts, weights] + sums, mixed)


def combine_keep_kernel(parts_ref, weights_ref, far_ref, out_ref, near_ref, sem):
    copy = pltpu.make_async_copy(far_ref, near_ref, sem)
    copy.start()
    step = 8 * LANES
    for at in range(0, out_ref.shape[1], step):
        cols = slice(at, at + step)
        out_ref[:, cols] = weighed(parts_ref[:, cols], weights_ref[...]).astype(BF16)
    copy.wait()


def combine_keep(parts, weights, far):
    return pl.pallas_call(
        combine_keep_kernel,
        out_shape=(
            pltpu.VMEM((weights.shape[0] // 2, parts.shape[1]), BF16),
            pltpu.VMEM(far.shape, BF16),
        ),
        in_specs=[VMEM, VMEM, pl.BlockSpec(memory_space=pl.ANY)],
        out_specs=(VMEM, VMEM),
        scratch_shapes=[pltpu.SemaphoreType.DMA],
        compiler_params=pltpu.CompilerParams(vmem_limit_bytes=8 << 20),
        name="combine_keep",
    )(resident(parts), weights, pltpu.with_memory_space_constraint(far, pltpu.HBM))


def join(first, others):
    if not others:
        return first

    def body(held):
        return sum(part.astype(F32) for part in held).astype(BF16)

    return stream(body, [first] + others, [], first.shape[0], keep=False)


def expert_kernel(count, ups, downs, *refs):
    sources = refs[:count]
    up_hbm, down_hbm = refs[count : count + 2]
    outs = refs[count + 2 : 2 * count + 2]
    up_ref, down_ref, hidden_ref, made_ref, sems, out_sems = refs[2 * count + 2 :]
    each, _ = sources[0].shape
    copies = [
        pltpu.make_async_copy(
            hbm.at[:, pl.ds(start, size)], ref.at[:, pl.ds(start, size)], sems.at[base + n]
        )
        for hbm, ref, blocks, base in (
            (up_hbm, up_ref, ups, 0),
            (down_hbm, down_ref, downs, len(ups)),
        )
        for n, (start, size) in enumerate(blocks)
    ]
    for copy in copies:
        copy.start()
    if count == 1:
        rows = sources[0][...]
    else:
        rows = jnp.concatenate([source[...] for source in sources], 0)
    tile = 2 * LANES
    for (start, size), copy in zip(ups, copies):
        copy.wait()
        for at in range(start, start + size, tile):
            cols = slice(at, min(at + tile, start + size))
            lifted = jnp.dot(rows, up_ref[:, cols], preferred_element_type=F32)
            hidden_ref[:, cols] = (lifted / (1.0 + jnp.exp(-lifted))).astype(BF16)
    hidden = hidden_ref[...]
    tile = 4 * LANES
    flying = []
    for n, ((start, size), copy) in enumerate(zip(downs, copies[len(ups) :])):
        copy.wait()
        for at in range(start, start + size, tile):
            cols = slice(at, at + tile)
            made_ref[:, cols] = jnp.dot(
                hidden, down_ref[:, cols], preferred_element_type=F32
            ).astype(BF16)
        for k in range(count):
            cols = pl.ds(start, size)
            flying.append(
                pltpu.make_async_copy(
                    made_ref.at[pl.ds(k * each, each), cols],
                    outs[k].at[:, cols],
                    out_sems.at[k, n],
                )
            )
            flying[-1].start()
    for copy in flying:
        copy.wait()


def blocks_of(total, shares):
    unit = total // sum(shares)
    if unit % LANES or unit * sum(shares) != total:
        return [(0, total)]
    ends = [unit * sum(shares[: n + 1]) for n in range(len(shares))]
    return [(end - unit * share, unit * share) for end, share in zip(ends, shares)]


def apply_expert(chunks, up_local, down_local):
    count = len(chunks)
    each, width = chunks[0].shape
    hidden = up_local.shape[1]
    anywhere = pl.BlockSpec(memory_space=pl.ANY)
    ups = blocks_of(hidden, UP_SHARES)
    downs = blocks_of(width, DOWN_SHARES)
    return pl.pallas_call(
        functools.partial(expert_kernel, count, ups, downs),
        out_shape=[pltpu.HBM((each, width), BF16)] * count,
        in_specs=[VMEM] * count + [anywhere] * 2,
        out_specs=[anywhere] * count,
        scratch_shapes=[
            pltpu.VMEM(up_local.shape, BF16),
            pltpu.VMEM(down_local.shape, BF16),
            pltpu.VMEM((count * each, hidden), BF16),
            pltpu.VMEM((count * each, width), BF16),
            pltpu.SemaphoreType.DMA((len(ups) + len(downs),)),
            pltpu.SemaphoreType.DMA((count, len(downs))),
        ],
        cost_estimate=pl.CostEstimate(
            flops=4 * count * each * width * hidden,
            bytes_accessed=4 * width * hidden + 4 * count * each * width,
            transcendentals=count * each * hidden,
        ),
        compiler_params=pltpu.CompilerParams(vmem_limit_bytes=50 << 20),
        name="expert",
    )(
        *[resident(chunk) for chunk in chunks],
        pltpu.with_memory_space_constraint(up_local, pltpu.HBM),
        pltpu.with_memory_space_constraint(down_local, pltpu.HBM),
    )


def local(
    tokens,
    queries,
    keys_values,
    scan_input,
    state_maps,
    step_size,
    step_decay,
    block_pool,
    state_pool,
    block_holder,
    block_index,
    cached_blocks,
    state_holder,
    state_index,
    norm_gain,
    router_weight,
    expert_ids,
    up_weight,
    down_weight,
):
    peers = lax.axis_size("dp")
    columns = lax.axis_size("expert")
    near = peers // 2

    def route(turn, side):
        return [
            (h * near + i, (h + side) % 2 * near + (i + turn) % near)
            for h in range(2)
            for i in range(near)
        ]

    def move(rows, turn, side):
        return lax.ppermute(rows, "dp", route(turn, side))

    def swap_rows(rows):
        blocks = rows.reshape(columns, -1, rows.shape[-1])
        moved = lax.all_to_all(blocks, "expert", split_axis=0, concat_axis=0, tiled=True)
        return moved.reshape(rows.shape)

    slot = block_holder.shape[1] // peers
    count = 2 * expert_ids.shape[0]
    ask, known = plan(peers, block_holder, block_index, cached_blocks, state_index, expert_ids.T)
    asked = lax.all_to_all(ask, "dp", split_axis=0, concat_axis=0, tiled=True)[:, 0]
    place = lax.axis_index("dp")

    def source_of(turn):
        return (place // near + 1) % 2 * near + (place % near + near - turn) % near

    states = state_pool.reshape(state_pool.shape[0], -1, LANES).astype(BF16)
    packed = pack(asked[:, count : count + slot + 1], block_pool, states)
    got = lax.all_to_all(packed, "dp", split_axis=0, concat_axis=0, tiled=True)

    router = router_weight.T
    sums, from_inputs, fade, keep = scan_local(
        scan_input, state_maps, step_size, step_decay, tokens
    )
    own = jnp.asarray(place)[None]
    (own_pick,) = picks(own, asked, tokens.shape[0], router_weight.shape[1])
    mixed, normed, send, final_state = mix(
        state_holder, queries, keys_values, got, known, sums, from_inputs, fade, keep, state_maps,
        norm_gain[None, :], own_pick,
    )
    up_local, down_local = up_weight[0], down_weight[0]

    far_rows = [move(normed, 0, 1)]
    near_in = swap_rows(send)
    near_moved = [move(near_in, turn, 0) for turn in range(1, near)]
    far_rows += [move(far_rows[0], turn, 0) for turn in range(1, near)]
    far_in, far_weights = [], []
    for turn in range(near):
        chosen, far_gates = choose(source_of(turn)[None], far_rows[turn], asked, router)
        far_in.append(swap_rows(chosen))
        far_weights.append(far_gates)

    weights = gates(own, normed, asked, router)

    def experts_on(rows):
        return list(apply_expert(rows, up_local, down_local))

    near_out, first_out = experts_on([near_in, far_in[0]])
    moved_out, far_out = [], [first_out]
    if near > 1:
        late = experts_on(near_moved + far_in[1:])
        moved_out, far_out = late[: near - 1], far_out + late[near - 1 :]

    far_sums = []
    for turn in range(near):
        back = swap_rows(far_out[turn])
        if turn > 0 and turn == near - 1:
            part, near_out = combine_keep(back, far_weights[turn], near_out)
        else:
            part = combine(back, far_weights[turn])
        far_sums.append(move(part, near - turn, 1))
    moved_back = [move(rows, near - turn, 0) for turn, rows in enumerate(moved_out, 1)]
    joined = join(near_out, moved_back)
    near_back = swap_rows(joined)
    layer_out = finish(near_back, weights, far_sums, mixed)
    return (layer_out, final_state.reshape(1, -1))


def solution(mesh):
    placed = (
        P(("dp", "expert"), None),
        P(("dp", "expert"), None),
        P(("dp", "expert"), None),
        P(("dp", "expert"), None),
        P(("dp", "expert"), None),
        P(("dp", "expert"), None),
        P(("dp", "expert"), None),
        P(("dp", "expert"), None, None),
        P(("dp", "expert"), None),
        P(("dp", "expert"), None),
        P(("dp", "expert"), None),
        P(("dp", "expert")),
        P(("dp", "expert")),
        P(("dp", "expert")),
        P(),
        P(),
        P(("dp", "expert"), None),
        P("expert", None, "dp"),
        P("expert", "dp", None),
    )
    return jax.shard_map(
        local,
        mesh=mesh,
        in_specs=placed,
        out_specs=(P(("dp", "expert"), None), P(("dp", "expert"), None)),
        check_vma=False,
    )
```
